256 devices in a mesh: mem: 128 (over z, x, y), tp: 2 (over core).
Axes of the slice: x: 4, y: 4, z: 8, core: 2. Of those that a mesh axis runs over, the one named last changes fastest.
Arguments:
- queries: bfloat16 [65536, 2048], P('mem', 'tp')
- local_keys: bfloat16 [65536, 2048], P('mem', 'tp')
- local_values: bfloat16 [65536, 2048], P('mem', 'tp'), may hold values from -6 to 6
- mem_keys: bfloat16 [131072, 2048], P('mem', 'tp')
- mem_values: bfloat16 [131072, 2048], P('mem', 'tp'), may hold values from -6 to 6
- gate_bias: float32 [16], P('tp'), may hold values from -2 to 2
- out_weight: bfloat16 [2048, 2048], P('tp'), may hold values from -0.125 to 0.125
- block_ids: int32 [128, 16, 16], replicated, may hold values from 0 to 1023, as said below
- block_home: int32 [1024], replicated, may hold values from 0 to 1023, as said below
Outputs:
- mixed: bfloat16 [65536, 2048], P(('mem', 'tp'))
The draws below stay inside these ranges and needn't reach their ends.
Inputs may be any that keep to these rules, and one draw needn't show every extreme that they name: `block_ids`: block_home is a permutation of the block ids. Let the holder of a block b be block_home[b] // 8. For each sequence block and each group of 8 heads starting at a multiple of 8, at most 2 of the group's 8 * 16 listed entries have the same holder, and some holder has exactly 2 of them. Ids may repeat within a list. `block_home`: A permutation of the block ids.
All inputs are finite; a program needn't handle non-finite values.
Results may differ from the reference program's by a relative error of at most 0.0057.
Values may be sent and summed in bfloat16 or wider, within the bound.
A program may use at most 128 MiB of HBM per device.

```python
import math
import jax
import jax.numpy as jnp
from jax import lax

D = 2048
HEADS = 16
HD = 128
SPAN = 512
BLK = 128
TOPK = 16
MB_DEV = 8
HL = 8
CAP = 2
N_SPANS = 128
TOKENS = 65536
NBLOCKS = 1024
MEM_ROWS = 131072


def draw_queries(key, part):
    result = jax.random.truncated_normal(jax.random.fold_in(key, 1), -6.0, 6.0, (TOKENS, D))
    return result.astype(jnp.bfloat16)


def draw_local_keys(key, part):
    result = jax.random.truncated_normal(jax.random.fold_in(key, 5), -6.0, 6.0, (TOKENS, D))
    return result.astype(jnp.bfloat16)


def draw_mem_keys(key, part):
    result = jax.random.truncated_normal(jax.random.fold_in(key, 7), -6.0, 6.0, (MEM_ROWS, D))
    return result.astype(jnp.bfloat16)


def routing(key):
    base_key = jax.random.fold_in(key, 101)
    inverse_key, list_key = jax.random.split(base_key, 2)
    inverse = jax.random.permutation(inverse_key, NBLOCKS).astype(jnp.int32)
    home_table = jnp.argsort(inverse, stable=True).astype(jnp.int32)
    halves = HEADS // HL
    request_count = HL * TOPK

    def one_list(list_index):
        list_seed = jax.random.fold_in(list_key, list_index)
        first_key, second_key, third_key = jax.random.split(list_seed, 3)
        items = jax.random.permutation(first_key, N_SPANS * CAP).astype(jnp.int32)
        holders = items % N_SPANS
        leading = holders[0]
        order = jnp.argsort((holders != leading).astype(jnp.int32), stable=True)
        chosen = holders[order][:request_count]
        chosen = jax.random.permutation(second_key, chosen)
        local_block = jax.random.randint(third_key, (request_count,), 0, MB_DEV, dtype=jnp.int32)
        return inverse[chosen * MB_DEV + local_block]
    id_lists = jax.vmap(one_list)(jnp.arange(N_SPANS * halves, dtype=jnp.int32))
    id_lists = id_lists.reshape(N_SPANS, halves, HL, TOPK).reshape(N_SPANS, HEADS, TOPK)
    return (home_table, id_lists.astype(jnp.int32))


def draw_block_ids(key, part):
    return routing(key)[1]


def draw_block_home(key, part):
    return routing(key)[0]


def levels(own_key, dims, cuts, smallest, high):
    def one(position, blocks):
        heights = jax.random.uniform(jax.random.fold_in(jax.random.fold_in(own_key, 6), position), (blocks,), jnp.float32, smallest / len(cuts), high / len(cuts))
        return jnp.repeat(jnp.exp(heights), dims[position] // blocks).reshape((-1,) + (1,) * (len(dims) - position - 1))

    level = one(*cuts[0])
    for cut in cuts[1:]:
        level = level * one(*cut)
    return level


def noise(rng, dims, scale, bound, shards=(), held_as=jnp.bfloat16):
    values = scale * jax.random.normal(rng, dims, jnp.float32)
    if shards:
        values = values * levels(rng, dims, shards, -0.22, 0.18)
    return jnp.clip(values, -bound, bound).astype(held_as)


def setup_inputs(seed: int = 0) -> dict:
    seeds = jax.random.split(jax.random.key(seed), 10)
    return {
        "queries": draw_queries(jax.random.fold_in(seeds[9], 71), 0),
        "local_keys": draw_local_keys(jax.random.fold_in(seeds[9], 71), 0),
        "local_values": noise(seeds[2], (TOKENS, D), 1.0, 6.0, ((0, 128), (1, 2))),
        "mem_keys": draw_mem_keys(jax.random.fold_in(seeds[9], 71), 0),
        "mem_values": noise(seeds[4], (MEM_ROWS, D), 1.0, 6.0, ((0, 128), (1, 2))),
        "gate_bias": jnp.clip(jax.random.uniform(seeds[5], (HEADS,), jnp.float32, -2.0, 2.0) * levels(seeds[5], (HEADS,), ((0, 2),), -0.4, 0.0), -2.0, 2.0),
        "out_weight": noise(seeds[6], (D, D), D ** -0.5, 0.125, ((0, 2),)),
        "block_ids": draw_block_ids(jax.random.fold_in(seeds[9], 71), 0),
        "block_home": draw_block_home(jax.random.fold_in(seeds[9], 71), 0),
    }


def softmax_rows(scores):
    highest = lax.optimization_barrier(jnp.max(scores, axis=-1, keepdims=True))
    exponent = jnp.exp(scores - highest)
    return exponent / lax.optimization_barrier(jnp.sum(exponent, axis=-1, keepdims=True))

def round_weights(weights):
    rounded = lax.optimization_barrier(weights.astype(jnp.bfloat16))
    return rounded.astype(jnp.float32)

def reference(queries, local_keys, local_values, mem_keys, mem_values, gate_bias, out_weight, block_ids, block_home):
    factor = 1.0 / math.sqrt(HD)
    key_blocks = mem_keys.reshape(NBLOCKS, BLK, HEADS, HD)
    value_blocks = mem_values.reshape(NBLOCKS, BLK, HEADS, HD)
    positions = jnp.arange(SPAN, dtype=jnp.int32)
    causal = positions[:, None] >= positions[None, :]
    mixing = jax.nn.sigmoid(gate_bias.astype(jnp.float32))[None, :, None]
    head_index = jnp.arange(HEADS, dtype=jnp.int32)[:, None]

    def one_span(span_index):
        first_row = (span_index * SPAN).astype(jnp.int32)
        query_rows = lax.dynamic_slice_in_dim(queries, first_row, SPAN, 0).reshape(SPAN, HEADS, HD).astype(jnp.float32)
        near_keys = lax.dynamic_slice_in_dim(local_keys, first_row, SPAN, 0).reshape(SPAN, HEADS, HD).astype(jnp.float32)
        near_values = lax.dynamic_slice_in_dim(local_values, first_row, SPAN, 0).reshape(SPAN, HEADS, HD).astype(jnp.float32)
        home_slots = jnp.take(block_home, block_ids[span_index], axis=0).astype(jnp.int32)
        far_keys = key_blocks[home_slots, :, head_index, :].reshape(HEADS, TOPK * BLK, HD).astype(jnp.float32)
        far_values = value_blocks[home_slots, :, head_index, :].reshape(HEADS, TOPK * BLK, HD).astype(jnp.float32)
        far_scores = jnp.einsum('qhd,hkd->hqk', query_rows, far_keys) * factor
        far_weights = round_weights(softmax_rows(far_scores))
        remote = jnp.einsum('hqk,hkd->qhd', far_weights, far_values)
        near_scores = jnp.einsum('qhd,khd->hqk', query_rows, near_keys) * factor
        near_scores = jnp.where(causal[None, :, :], near_scores, -1e+30)
        near_weights = round_weights(softmax_rows(near_scores))
        nearby = jnp.einsum('hqk,khd->qhd', near_weights, near_values)
        combined = (mixing * remote + (1.0 - mixing) * nearby).astype(jnp.bfloat16).reshape(SPAN, D)
        return jnp.dot(combined, out_weight, preferred_element_type=jnp.float32).astype(jnp.bfloat16)
    mixed = lax.map(one_span, jnp.arange(N_SPANS, dtype=jnp.int32))
    return mixed.reshape(TOKENS, D)
```

```python
import functools
import math

import jax
import jax.numpy as jnp
from jax import lax
from jax.experimental import pallas as pl
from jax.experimental.pallas import tpu as pltpu
from jax.sharding import PartitionSpec as P

HD = 128
BLK = 128
TOPK = 16
PLANES = 8
SIDE = 16
HL = 8
GROUPS = 2
HG = HL // GROUPS
MB = 8
ROWS = BLK // SIDE
OWN = SIDE * MB * HG
CAPS = (344, 280, 200, 88)
OFFS = (0, 344, 624, 824)
CSUM = 912
NPIECE = OWN + 2 * CSUM
LPAD = 384
SLOTS = HG * TOPK
MESH = pl.DeviceIdType.MESH
F32 = jnp.float32
BF16 = jnp.bfloat16
SCALE = math.log2(math.e) / math.sqrt(HD)


def iota(shape, axis):
    return lax.broadcasted_iota(jnp.int32, shape, axis)


def hot(mask):
    return jnp.where(mask, 1.0, 0.0).astype(BF16)


def dot(a, b, dims):
    return lax.dot_general(a, b, (dims, ((), ())), preferred_element_type=F32)


def ways(dz, even):
    up = ((dz >= 1) & (dz <= 3)) | ((dz == 4) & even)
    down = (dz >= 5) | ((dz == 4) & jnp.logical_not(even))
    return up, down


def plan_kernel(plane_ref, ids_ref, home_ref, lists_ref, dest_ref, ok_ref, need, hi_s, code_s, rank_s):
    lane = iota((1, 2048), 1)
    head = (lane >> 4) & 7
    head_term = (head >> 2) * 128 + (head & 3) * 8

    def one_row(row, carry):
        ids = ids_ref[pl.ds(row, 1), :]
        by_hi = hot(iota((32, 2048), 0) == (ids >> 5))
        both = dot(home_ref[...], by_hi, ((1,), (0,)))
        at_lo = iota((32, 2048), 0) == (ids & 31)
        pos_hi = jnp.sum(jnp.where(at_lo, both[:32], 0.0), axis=0, keepdims=True).astype(jnp.int32)
        pos_lo = jnp.sum(jnp.where(at_lo, both[32:], 0.0), axis=0, keepdims=True).astype(jnp.int32)
        code = (pos_lo >> 3) * 32 + head_term + (pos_lo & 7)
        count = dot(
            hot(iota((32, 2048), 0) == pos_hi), hot(iota((256, 2048), 0) == code), ((1,), (1,))
        )
        need[row] = count
        hi_s[pl.ds(row, 1), :] = pos_hi
        code_s[pl.ds(row, 1), :] = code
        return carry

    lax.fori_loop(0, 16, one_row, 0)

    row_plane = iota((32, 256), 0) >> 2
    even = (iota((32, 256), 1) & 1) == 0
    r, s = iota((256, 256), 0), iota((256, 256), 1)
    same_group = (r >> 7) == (s >> 7)
    prefix = hot(same_group & (r <= s))
    whole = hot(same_group)
    same_plane = (r >> 2) == (s >> 2)
    rows_before = hot(same_plane & (s < r))
    rows_all = hot(same_plane)
    over = jnp.zeros((32, 256), F32)
    ranks_all = []
    for side in range(2):
        far = [jnp.zeros((32, 256), jnp.int32), jnp.zeros((32, 256), jnp.int32)]
        for zr in range(PLANES):
            wanted = need[side * PLANES + zr] > 0.5
            dz = (zr - row_plane) & 7
            up, down = ways(dz, even)
            far[0] = jnp.maximum(far[0], jnp.where(wanted & up, dz, 0))
            far[1] = jnp.maximum(far[1], jnp.where(wanted & down, 8 - dz, 0))
        levels = jnp.concatenate(
            [jnp.where(far[way] == d, 1.0, 0.0) for way in range(2) for d in (4, 3, 2, 1)], axis=0
        )
        level_hot = levels.astype(BF16)
        before_lane = dot(level_hot, prefix, ((1,), (0,)))
        row_total = dot(level_hot, whole, ((1,), (0,))).astype(BF16)
        before_row = dot(rows_before, row_total, ((1,), (0,)))
        plane_total = dot(rows_all, row_total, ((1,), (0,)))
        for way in range(2):
            base = jnp.zeros((32, 256), F32)
            rank = jnp.zeros((32, 256), F32)
            for e in range(4):
                part = slice((way * 4 + e) * 32, (way * 4 + e) * 32 + 32)
                rank = rank + levels[part] * (base + before_row[part] + before_lane[part])
                base = base + plane_total[part]
                over = jnp.maximum(over, base - float(CAPS[3 - e]))
            if side == 0:
                ranks_all.append(rank.astype(jnp.int32) - 1)
                for p in range(PLANES):
                    rank_s[way, p] = ranks_all[way][p * 4 : p * 4 + 4]
    ok_ref[...] = jnp.broadcast_to(jnp.max(over, keepdims=True), (8, 128))

    plane = plane_ref[0]
    values = jnp.where(iota((8, 128), 0) == 0, iota((8, 128), 1), 1).astype(F32).astype(BF16)
    for way in range(2):
        mine = rank_s[way, plane]
        for g in range(GROUPS):
            index = jnp.zeros((1, LPAD), F32)
            for rr in range(4):
                ranks = mine[rr : rr + 1, g * 128 : g * 128 + 128]
                got = dot(values, hot(iota((LPAD, 128), 0) == ranks), ((1,), (1,)))
                index = index + got[0:1] + got[1:2] * float(rr * 128)
            lists_ref[way * GROUPS + g : way * GROUPS + g + 1, :] = index.astype(jnp.int32)

    dz = (plane - row_plane) & 7
    up, down = ways(dz, even)
    address = (iota((32, 256), 0) & 3) * 128 + (iota((32, 256), 1) & 127)
    for d in range(1, 5):
        address = jnp.where(up & (dz == d), ranks_all[0] + (OWN + OFFS[d - 1]), address)
        address = jnp.where(down & (8 - dz == d), ranks_all[1] + (OWN + CSUM + OFFS[d - 1]), address)
    digits = jnp.concatenate([address >> 5, address & 31], axis=1).astype(F32).astype(BF16)
    by_hi = hot(iota((32, 2048), 0) == hi_s[pl.ds(plane, 1), :])
    found = dot(digits, by_hi, ((0,), (0,)))
    at_code = iota((256, 2048), 0) == code_s[pl.ds(plane, 1), :]
    dest_hi = jnp.sum(jnp.where(at_code, found[:256], 0.0), axis=0, keepdims=True)
    dest_lo = jnp.sum(jnp.where(at_code, found[256:], 0.0), axis=0, keepdims=True)
    dest_ref[...] = (dest_hi * 32.0 + dest_lo).astype(jnp.int32)


def make_plan(block_ids, block_home, plane, tp_index):
    ids = block_ids.reshape(PLANES, SIDE, 2, HL, TOPK).transpose(2, 0, 1, 3, 4).reshape(2, PLANES, 2048)
    ids = jnp.where(tp_index == 0, ids, ids[::-1]).reshape(2 * PLANES, 2048)
    home = block_home.reshape(32, 32).T
    home = jnp.concatenate([home >> 5, home & 31], axis=0).astype(BF16)
    vmem = pl.BlockSpec(memory_space=pltpu.VMEM)
    return pl.pallas_call(
        plan_kernel,
        out_shape=(
            jax.ShapeDtypeStruct((4, LPAD), jnp.int32),
            jax.ShapeDtypeStruct((1, 2048), jnp.int32),
            jax.ShapeDtypeStruct((8, 128), F32),
        ),
        in_specs=[pl.BlockSpec(memory_space=pltpu.SMEM), vmem, vmem],
        out_specs=(vmem, vmem, vmem),
        scratch_shapes=[
            pltpu.VMEM((16, 32, 256), F32),
            pltpu.VMEM((16, 2048), jnp.int32),
            pltpu.VMEM((16, 2048), jnp.int32),
            pltpu.VMEM((2, PLANES, 4, 256), jnp.int32),
        ],
        compiler_params=pltpu.CompilerParams(vmem_limit_bytes=48 << 20),
        name="plan",
    )(plane.reshape(1), ids, home)


def pick(index, rows, width, base, data):
    def kernel(index_ref, data_ref, out_ref):
        for n, row in enumerate(rows):

            def one(j, carry):
                out_ref[0, n * width + j] = data_ref[0, index_ref[row, base + j]]
                return carry

            lax.fori_loop(0, width, one, 0, unroll=8)

    count = len(rows) * width
    return pl.pallas_call(
        kernel,
        grid=(2,),
        out_shape=jax.ShapeDtypeStruct((2, count, ROWS, HD), BF16),
        in_specs=[
            pl.BlockSpec(memory_space=pltpu.SMEM),
            pl.BlockSpec((1,) + data.shape[1:], lambda i: (i, 0, 0, 0)),
        ],
        out_specs=pl.BlockSpec((1, count, ROWS, HD), lambda i: (i, 0, 0, 0)),
        compiler_params=pltpu.CompilerParams(vmem_limit_bytes=48 << 20),
        name="pick",
    )(index, data)


def place():
    mem = lax.axis_index("mem")
    plane, me = mem // SIDE, mem % SIDE
    above = ((plane + 1) % PLANES) * SIDE + me
    below = ((plane + PLANES - 1) % PLANES) * SIDE + me
    return plane, me, lax.axis_index("tp"), (above, below)


def greet(ring):
    plane, me, tp, nexts = place()
    barrier = pltpu.get_barrier_semaphore()

    def one(k, carry):
        peer = plane * SIDE + (me + k) % SIDE
        pl.semaphore_signal(barrier, inc=1, device_id=(peer, tp), device_id_type=MESH)
        return carry

    lax.fori_loop(1, SIDE, one, 0)
    if ring:
        for peer in nexts:
            pl.semaphore_signal(barrier, inc=1, device_id=(peer, tp), device_id_type=MESH)
    pl.semaphore_wait(barrier, SIDE - 1 + (2 if ring else 0))


def spread(g, sources, own, send, recv):
    plane, me, tp, _ = place()
    for kv in range(2):

        def to_peer(k, carry):
            i = (me + k) % SIDE
            for h in range(HG):
                pltpu.make_async_remote_copy(
                    src_ref=sources[kv].at[:, i, :, pl.ds((g * HG + h) * HD, HD)],
                    dst_ref=own.at[kv, pl.ds(me * (HG * MB) + h * MB, MB)],
                    send_sem=send.at[kv],
                    recv_sem=recv.at[kv],
                    device_id=(plane * SIDE + i, tp),
                    device_id_type=MESH,
                ).start()
            return carry

        lax.fori_loop(1, SIDE, to_peer, 0)
        for h in range(HG):
            pltpu.make_async_copy(
                sources[kv].at[:, me, :, pl.ds((g * HG + h) * HD, HD)],
                own.at[kv, pl.ds(me * (HG * MB) + h * MB, MB)],
                recv.at[kv],
            ).start()


def spread_wait(own, send, recv):
    for kv in range(2):
        pltpu.make_async_copy(own.at[kv], own.at[kv], recv.at[kv]).wait()
        sent = own.at[kv, pl.ds(0, (SIDE - 1) * HG * MB)]
        pltpu.make_async_copy(sent, sent, send.at[kv]).wait()


def hop_copy(lst, pool, send, recv, kv, way, d):
    _, _, tp, nexts = place()
    count = CAPS[d]
    base = OWN + way * CSUM
    if d == 0:
        source = lst.at[kv, pl.ds(way * CAPS[0], count)]
    else:
        source = pool.at[kv, pl.ds(base + OFFS[d - 1], count)]
    return pltpu.make_async_remote_copy(
        src_ref=source,
        dst_ref=pool.at[kv, pl.ds(base + OFFS[d], count)],
        send_sem=send.at[kv, way, d],
        recv_sem=recv.at[kv, way, d],
        device_id=(nexts[way], tp),
        device_id_type=MESH,
    )


def hop(args, d):
    for kv in range(2):
        for way in range(2):
            if d > 0:
                hop_copy(*args, kv, way, d - 1).wait_recv()
            if d < 4:
                hop_copy(*args, kv, way, d).start()


def hops_sent(args):
    for kv in range(2):
        for way in range(2):
            for d in range(4):
                hop_copy(*args, kv, way, d).wait_send()


def deliver(given, rcv, send, recv):
    plane, me, tp, _ = place()
    for kv in range(2):

        def to_peer(k, carry):
            i = (me + k) % SIDE
            pltpu.make_async_remote_copy(
                src_ref=given.at[kv, pl.ds(i * SLOTS, SLOTS)],
                dst_ref=rcv.at[kv, me],
                send_sem=send.at[kv],
                recv_sem=recv.at[kv],
                device_id=(plane * SIDE + i, tp),
                device_id_type=MESH,
            ).start()
            return carry

        lax.fori_loop(1, SIDE, to_peer, 0)
        pltpu.make_async_copy(given.at[kv, pl.ds(me * SLOTS, SLOTS)], rcv.at[kv, me], recv.at[kv]).start()


def deliver_sent(given, send):
    for kv in range(2):
        sent = given.at[kv, pl.ds(0, (SIDE - 1) * SLOTS)]
        pltpu.make_async_copy(sent, sent, send.at[kv]).wait()


def softmax_dot(query, keys, visible):
    scores = dot(query, keys, ((1,), (1,)))
    if visible is not None:
        scores = jnp.where(visible, scores, -1e30)
    highest = jnp.max(scores, axis=1, keepdims=True)
    exponent = jnp.exp2((scores - highest) * SCALE)
    return (exponent * (1.0 / jnp.sum(exponent, axis=1, keepdims=True))).astype(BF16)


def columns(h):
    return pl.ds(pl.multiple_of(h * HD, HD), HD)


def attend_near(g, q_ref, k_ref, v_ref, near):
    def one(h, carry):
        cols = columns(g * HG + h)
        for rb in range(4):
            rows = pl.ds(rb * 128, 128)
            width = (rb + 1) * 128
            visible = iota((128, width), 0) + rb * 128 >= iota((128, width), 1)
            part = softmax_dot(q_ref[rows, cols], k_ref[pl.ds(0, width), cols], visible)
            near[rows, columns(h)] = dot(part, v_ref[pl.ds(0, width), cols], ((1,), (0,)))
        return carry

    lax.fori_loop(0, HG, one, 0)


def tile(rcv, kv, h):
    rows = rcv[kv, :, pl.ds(pl.multiple_of(h * TOPK, TOPK), TOPK)]
    return rows.astype(F32).reshape(SIDE * TOPK * ROWS, HD).astype(BF16)


def attend_keys(g, q_ref, rcv, recv, weights):
    pltpu.make_async_copy(rcv.at[0], rcv.at[0], recv.at[0]).wait()

    def one(h, carry):
        keys = tile(rcv, 0, h)
        cols = columns(g * HG + h)

        def block(rb, inner):
            rows = pl.ds(pl.multiple_of(rb * 128, 128), 128)
            weights[h, rows, :] = softmax_dot(q_ref[rows, cols], keys, None)
            return inner

        return lax.fori_loop(0, 4, block, carry)

    lax.fori_loop(0, HG, one, 0)


def attend_values(g, gate_ref, rcv, recv, weights, near, out_ref):
    pltpu.make_async_copy(rcv.at[1], rcv.at[1], recv.at[1]).wait()

    def one(h, carry):
        remote = dot(weights[h], tile(rcv, 1, h), ((1,), (0,)))
        gate = gate_ref[g * HG + h]
        out_ref[:, columns(h)] = (gate * remote + (1.0 - gate) * near[:, columns(h)]).astype(BF16)
        return carry

    lax.fori_loop(0, HG, one, 0)


def kernel_spread(mem_keys, mem_values, own, s1_send, s1_recv):
    greet(False)
    spread(0, (mem_keys, mem_values), own, s1_send, s1_recv)
    spread_wait(own, s1_send, s1_recv)


def kernel_ring(mem_keys, mem_values, own, lst, pool, own_next, *sems):
    s1_send, s1_recv, z_send, z_recv, copied = sems
    args = (lst, pool, z_send, z_recv)
    greet(True)
    hop(args, 0)
    spread(1, (mem_keys, mem_values), own_next, s1_send, s1_recv)
    keep = pltpu.make_async_copy(own, pool.at[:, pl.ds(0, OWN)], copied)
    keep.start()
    for d in range(1, 5):
        hop(args, d)
    spread_wait(own_next, s1_send, s1_recv)
    hops_sent(args)
    keep.wait()


def kernel_ring_attend(
    gate_ref, own, lst, given, q_ref, k_ref, v_ref, pool, out_ref, rcv, weights, near, *sems
):
    z_send, z_recv, s3_send, s3_recv, copied = sems
    args = (lst, pool, z_send, z_recv)
    greet(True)
    hop(args, 0)
    deliver(given, rcv, s3_send, s3_recv)
    keep = pltpu.make_async_copy(own, pool.at[:, pl.ds(0, OWN)], copied)
    keep.start()
    attend_near(0, q_ref, k_ref, v_ref, near)
    hop(args, 1)
    attend_keys(0, q_ref, rcv, s3_recv, weights)
    hop(args, 2)
    attend_values(0, gate_ref, rcv, s3_recv, weights, near, out_ref)
    hop(args, 3)
    hop(args, 4)
    hops_sent(args)
    deliver_sent(given, s3_send)
    keep.wait()


def kernel_attend(gate_ref, given, q_ref, k_ref, v_ref, out_ref, rcv, weights, near, s3_send, s3_recv):
    greet(False)
    deliver(given, rcv, s3_send, s3_recv)
    attend_near(1, q_ref, k_ref, v_ref, near)
    attend_keys(1, q_ref, rcv, s3_recv, weights)
    attend_values(1, gate_ref, rcv, s3_recv, weights, near, out_ref)
    deliver_sent(given, s3_send)


def fast_combined(lists, dest, gate, mem_keys, mem_values, queries, local_keys, local_values):
    smem = pl.BlockSpec(memory_space=pltpu.SMEM)
    hbm = pl.BlockSpec(memory_space=pl.ANY)
    vmem = pl.BlockSpec(memory_space=pltpu.VMEM)
    view = (MB, SIDE, ROWS, HL * HD)
    mem_keys, mem_values = mem_keys.reshape(view), mem_values.reshape(view)
    half = jax.ShapeDtypeStruct((queries.shape[0], HG * HD), BF16)
    own_shape = jax.ShapeDtypeStruct((2, OWN, ROWS, HD), BF16)
    pool_shape = jax.ShapeDtypeStruct((2, NPIECE, ROWS, HD), BF16)
    pair = pltpu.SemaphoreType.DMA((2,))
    ring = pltpu.SemaphoreType.DMA((2, 2, 4))
    one = pltpu.SemaphoreType.DMA
    attend_scratch = [
        pltpu.VMEM((2, SIDE, SLOTS, ROWS, HD), BF16),
        pltpu.VMEM((HG, 512, SIDE * TOPK * ROWS), BF16),
        pltpu.VMEM((512, HG * HD), F32),
    ]

    def call(kernel, name, number, outs, in_specs, out_specs, scratch, *args):
        return pl.pallas_call(
            kernel,
            out_shape=outs,
            in_specs=in_specs,
            out_specs=out_specs,
            scratch_shapes=scratch,
            compiler_params=pltpu.CompilerParams(
                collective_id=number, has_side_effects=True, vmem_limit_bytes=48 << 20
            ),
            name=name,
        )(*args)

    def far_lists(g, own):
        return pick(lists, (g, GROUPS + g), CAPS[0], 0, own)

    def requested(g, pool):
        return pick(dest, tuple(range(SIDE)), SLOTS, g * SLOTS, pool)

    own0 = call(
        kernel_spread, "spread", 0, own_shape, [hbm, hbm], hbm, [pair, pair], mem_keys, mem_values
    )
    lst0 = far_lists(0, own0)
    pool0, own1 = call(
        kernel_ring, "ring", 1, (pool_shape, own_shape), [hbm] * 4, (hbm, hbm),
        [pair, pair, ring, ring, one], mem_keys, mem_values, own0, lst0,
    )
    lst1 = far_lists(1, own1)
    given0 = requested(0, pool0)
    pool1, half0 = call(
        kernel_ring_attend, "ring_attend", 2, (pool_shape, half),
        [smem, hbm, hbm, hbm, vmem, vmem, vmem], (hbm, vmem),
        attend_scratch + [ring, ring, pair, pair, one],
        gate, own1, lst1, given0, queries, local_keys, local_values,
    )
    given1 = requested(1, pool1)
    half1 = call(
        kernel_attend, "attend", 3, half, [smem, hbm, vmem, vmem, vmem], vmem,
        attend_scratch + [pair, pair], gate, given1, queries, local_keys, local_values,
    )
    return half0, half1


def rank_within(owner_row):
    request_count = owner_row.shape[0]
    order_index = jnp.arange(request_count, dtype=jnp.int32)
    earlier = order_index[:, None] > order_index[None, :]
    same_owner = owner_row[:, None] == owner_row[None, :]
    return jnp.sum((same_owner & earlier).astype(jnp.int32), axis=1)


def slow_combined(gate, mem_keys, mem_values, queries, local_keys, local_values, block_ids, block_home):
    mem_count = lax.axis_size("mem")
    mem_index = lax.axis_index("mem")
    tp_index = lax.axis_index("tp")
    requests = HL * TOPK
    slots = 2
    group_ids = lax.dynamic_slice_in_dim(block_ids, tp_index * HL, HL, 1).reshape(mem_count, requests)
    home_slots = jnp.take(block_home, group_ids, axis=0)
    owners = home_slots // MB
    codes = (home_slots % MB) * HL + jnp.arange(requests, dtype=jnp.int32)[None, :] // TOPK
    own_owners = lax.dynamic_index_in_dim(owners, mem_index, 0, keepdims=False)
    own_codes = lax.dynamic_index_in_dim(codes, mem_index, 0, keepdims=False)
    own_ranks = rank_within(own_owners)
    slot_index = jnp.arange(slots, dtype=jnp.int32)
    owner_index = jnp.arange(mem_count, dtype=jnp.int32)
    matches = (own_owners[None, None, :] == owner_index[:, None, None]) & (
        own_ranks[None, None, :] == slot_index[None, :, None]
    )
    table = jnp.sum(jnp.where(matches, own_codes[None, None, :], 0), axis=2)
    wanted = lax.all_to_all(table, "mem", split_axis=0, concat_axis=0, tiled=True)
    flat_slot = own_owners * slots + own_ranks

    def fetch(rows):
        blocks = rows.reshape(MB, BLK, HL, HD)
        sent = blocks[wanted // HL, :, wanted % HL, :]
        got = lax.all_to_all(sent, "mem", split_axis=0, concat_axis=0, tiled=True)
        far = jnp.take(got.reshape(mem_count * slots, BLK, HD), flat_slot, axis=0)
        return far.reshape(HL, TOPK * BLK, HD)

    positions = jnp.arange(queries.shape[0], dtype=jnp.int32)
    causal = positions[:, None] >= positions[None, :]

    def by_head(x):
        return x.reshape(x.shape[0], HL, HD).transpose(1, 0, 2)

    def one_head(parts):
        q, far_k, far_v, near_k, near_v, g = parts
        remote = dot(softmax_dot(q, far_k, None), far_v, ((1,), (0,)))
        nearby = dot(softmax_dot(q, near_k, causal), near_v, ((1,), (0,)))
        return (g * remote + (1.0 - g) * nearby).astype(BF16)

    out = lax.map(
        one_head,
        (by_head(queries), fetch(mem_keys), fetch(mem_values), by_head(local_keys), by_head(local_values), gate),
    )
    out = out.reshape(GROUPS, HG, queries.shape[0], HD).transpose(0, 2, 1, 3)
    out = out.reshape(GROUPS, queries.shape[0], HG * HD)
    return out[0], out[1]


def per_device(
    queries, local_keys, local_values, mem_keys, mem_values, gate_bias, out_weight, block_ids, block_home
):
    mem_index = lax.axis_index("mem")
    tp_index = lax.axis_index("tp")
    gate = jax.nn.sigmoid(gate_bias)
    lists, dest, over = make_plan(block_ids, block_home, (mem_index // SIDE).astype(jnp.int32), tp_index)
    dest = dest.reshape(SIDE, HL * TOPK)
    half0, half1 = lax.cond(
        over[0, 0] <= 0.5,
        lambda: fast_combined(
            lists, dest, gate, mem_keys, mem_values, queries, local_keys, local_values
        ),
        lambda: slow_combined(
            gate, mem_keys, mem_values, queries, local_keys, local_values, block_ids, block_home
        ),
    )
    cut = HG * HD
    partial = jnp.dot(half0, out_weight[:cut], preferred_element_type=F32)
    partial = partial + jnp.dot(half1, out_weight[cut:], preferred_element_type=F32)
    mixed = lax.psum_scatter(partial, "tp", scatter_dimension=0, tiled=True)
    return mixed.astype(BF16)


def solution(mesh):
    in_specs = (
        P("mem", "tp"), P("mem", "tp"), P("mem", "tp"), P("mem", "tp"), P("mem", "tp"),
        P("tp"), P("tp", None), P(), P(),
    )
    return jax.shard_map(
        per_device, mesh=mesh, in_specs=in_specs, out_specs=P(("mem", "tp"), None), check_vma=False
    )
```

```python
import functools
import math

import jax
import jax.numpy as jnp
from jax import lax
from jax.experimental import pallas as pl
from jax.experimental.pallas import tpu as pltpu
from jax.sharding import PartitionSpec as P

HD = 128
BLK = 128
TOPK = 16
PLANES = 8
SIDE = 16
HL = 8
GROUPS = 2
HG = HL // GROUPS
MB = 8
ROWS = BLK // SIDE
OWN = SIDE * MB * HG
CAPS = (344, 280, 200, 88)
OFFS = (0, 344, 624, 824)
CSUM = 912
CUTS = (0, 88, 200, 280, 344)
NPIECE = OWN + 2 * CSUM
PIECE = 2 * ROWS
LPAD = 384
SLOTS = HG * TOPK
MESH = pl.DeviceIdType.MESH
F32 = jnp.float32
BF16 = jnp.bfloat16
SCALE = math.log2(math.e) / math.sqrt(HD)


def iota(shape, axis):
    return lax.broadcasted_iota(jnp.int32, shape, axis)


def hot(mask):
    return jnp.where(mask, 1.0, 0.0).astype(BF16)


def dot(a, b, dims):
    return lax.dot_general(a, b, (dims, ((), ())), preferred_element_type=F32)


def ways(dz, even):
    up = ((dz >= 1) & (dz <= 3)) | ((dz == 4) & even)
    down = (dz >= 5) | ((dz == 4) & jnp.logical_not(even))
    return up, down


def plan(ids_ref, home_ref, lists_ref, dest_ref, over_ref, rank_s, address_s, plane, tp):
    home = home_ref[...]
    home = jnp.concatenate([home >> 5, home & 31], axis=0).astype(F32).astype(BF16)
    lane = iota((1, 2048), 1)
    plane_term = ((lane & 127) >> 4) * 32
    row_plane = iota((32, 256), 0) >> 2
    even = (iota((32, 256), 1) & 1) == 0
    dz = ((iota((32, 256), 1) >> 5) - row_plane) & 7
    up, down = ways(dz, even)
    reach = (jnp.where(up, dz, 0), jnp.where(down, 8 - dz, 0))

    def find(side, h):
        block = ids_ref[side, h]
        ids = jnp.concatenate([block[q : q + 1] for q in range(TOPK)], axis=1)
        both = dot(home, hot(iota((128, 2048), 0) == (ids & 127)), ((1,), (0,)))
        at_hi = iota((8, 2048), 0) == (ids >> 7)
        pos_hi = jnp.sum(jnp.where(at_hi, both[:8], 0.0), axis=0, keepdims=True).astype(jnp.int32)
        pos_lo = jnp.sum(jnp.where(at_hi, both[8:], 0.0), axis=0, keepdims=True).astype(jnp.int32)
        return hot(iota((32, 2048), 0) == pos_hi), pos_lo

    r, s = iota((256, 256), 0), iota((256, 256), 1)
    same_group = (r >> 7) == (s >> 7)
    prefix = hot(same_group & (r <= s))
    whole = hot(same_group)
    same_plane = (r >> 2) == (s >> 2)
    rows_before = hot(same_plane & (s < r))
    rows_all = hot(same_plane)
    over = jnp.zeros((32, 256), F32)
    ranks = []
    for other in range(2):
        side = tp if other == 0 else 1 - tp

        def one_head(h, far):
            by_hi, pos_lo = find(side, h)
            count = dot(by_hi, hot(iota((256, 2048), 0) == plane_term + pos_lo), ((1,), (1,)))
            out = []
            for way in range(2):
                value = jnp.where(count > 0.5, reach[way], 0)
                for shift in (128, 64, 32):
                    value = jnp.maximum(value, pltpu.roll(value, shift, 1))
                out.append(jnp.where((iota((32, 256), 1) >> 5) == h, value, far[way]))
            return tuple(out)

        zero = jnp.zeros((32, 256), jnp.int32)
        far = lax.fori_loop(0, HL, one_head, (zero, zero))
        levels = jnp.concatenate(
            [jnp.where(far[way] == d, 1.0, 0.0) for way in range(2) for d in (4, 3, 2, 1)], axis=0
        )
        level_hot = levels.astype(BF16)
        before_lane = dot(level_hot, prefix, ((1,), (0,)))
        row_total = dot(level_hot, whole, ((1,), (0,))).astype(BF16)
        before_row = dot(rows_before, row_total, ((1,), (0,)))
        plane_total = dot(rows_all, row_total, ((1,), (0,)))
        for way in range(2):
            base = jnp.zeros((32, 256), F32)
            rank = jnp.zeros((32, 256), F32)
            for e in range(4):
                part = slice((way * 4 + e) * 32, (way * 4 + e) * 32 + 32)
                rank = rank + levels[part] * (base + before_row[part] + before_lane[part])
                base = base + plane_total[part]
                over = jnp.maximum(over, base - float(CAPS[3 - e]))
            if other == 0:
                ranks.append(rank.astype(jnp.int32) - 1)
                for p in range(PLANES):
                    rank_s[way, p] = ranks[way][p * 4 : p * 4 + 4]
    over_ref[...] = jnp.broadcast_to(jnp.max(over, keepdims=True), (8, 128))

    values = jnp.where(iota((8, 128), 0) == 0, iota((8, 128), 1), 1).astype(F32).astype(BF16)
    for way in range(2):
        mine = rank_s[way, plane]
        for g in range(GROUPS):
            index = jnp.zeros((1, LPAD), F32)
            for rr in range(4):
                wanted = mine[rr : rr + 1, g * 128 : g * 128 + 128]
                got = dot(values, hot(iota((LPAD, 128), 0) == wanted), ((1,), (1,)))
                index = index + got[0:1] + got[1:2] * float(rr * 128)
            lists_ref[g * 2 + way : g * 2 + way + 1, :] = index.astype(jnp.int32)

    dz = (plane - row_plane) & 7
    up, down = ways(dz, even)
    address = (iota((32, 256), 0) & 3) * 128 + (iota((32, 256), 1) & 127)
    for d in range(1, 5):
        address = jnp.where(up & (dz == d), ranks[0] + (OWN + OFFS[d - 1]), address)
        address = jnp.where(down & (8 - dz == d), ranks[1] + (OWN + CSUM + OFFS[d - 1]), address)
    high = jnp.transpose((address >> 5).astype(F32))
    low = jnp.transpose((address & 31).astype(F32))
    for h in range(HL):
        part = slice(h * 32, h * 32 + 32)
        address_s[h] = jnp.concatenate([high[part], low[part]], axis=0)

    def one_dest(h, carry):
        by_hi, pos_lo = find(tp, h)
        found = dot(address_s[h].astype(BF16), by_hi, ((1,), (0,)))
        at_lo = iota((32, 2048), 0) == pos_lo
        dest_hi = jnp.sum(jnp.where(at_lo, found[:32], 0.0), axis=0, keepdims=True)
        dest_lo = jnp.sum(jnp.where(at_lo, found[32:], 0.0), axis=0, keepdims=True)
        dest = (dest_hi * 32.0 + dest_lo).astype(jnp.int32)
        rows = jnp.concatenate([dest[:, q * 128 : q * 128 + 128] for q in range(TOPK)], axis=0)
        dest_ref[pl.ds(pl.multiple_of(h * TOPK, TOPK), TOPK), :] = rows
        return carry

    lax.fori_loop(0, HL, one_dest, 0)


def pick_list(g, lists_ref, own, out):
    for way in range(2):

        def one(j, carry):
            out[way * CAPS[0] + j] = own[lists_ref[g * 2 + way, j]]
            return carry

        lax.fori_loop(0, CAPS[0], one, 0, unroll=8)


def pick_requests(g, r, dest_ref, pool, out):
    column = (lax.axis_index("mem") // SIDE) * SIDE + r

    def one(j, carry):
        out[r * SLOTS + j] = pool[dest_ref[g * SLOTS + j, column]]
        return carry

    lax.fori_loop(0, SLOTS, one, 0, unroll=16)


def pick(name, list_group, request_group, lists, dest, own_next, own, ring):
    smem = pl.BlockSpec(memory_space=pltpu.SMEM)
    hbm = pl.BlockSpec(memory_space=pl.ANY)
    with_list, with_requests = own_next is not None, own is not None
    steps = 4

    def kernel(*refs):
        refs = list(refs)
        lists_ref, dest_ref = refs.pop(0), refs.pop(0)
        next_hbm = refs.pop(0) if with_list else None
        own_hbm, ring_hbm = (refs.pop(0), refs.pop(0)) if with_requests else (None, None)
        list_hbm = refs.pop(0) if with_list else None
        given_hbm = refs.pop(0) if with_requests else None
        in_sem, out_sem = refs.pop(), refs.pop()
        if with_list:
            next_v, list_v = refs.pop(0), refs.pop(0)
            next_in = pltpu.make_async_copy(next_hbm, next_v, in_sem.at[0])
            next_in.start()
        if with_requests:
            pool_v, given_v = refs.pop(0), refs.pop(0)
            own_in = pltpu.make_async_copy(own_hbm, pool_v.at[pl.ds(0, OWN)], in_sem.at[1])
            ring_in = pltpu.make_async_copy(ring_hbm, pool_v.at[pl.ds(OWN, 2 * CSUM)], in_sem.at[2])
            own_in.start()
            ring_in.start()
        outs = []
        if with_list:
            next_in.wait()
            pick_list(list_group, lists_ref, next_v, list_v)
            outs.append(pltpu.make_async_copy(list_v, list_hbm, out_sem.at[steps]))
            outs[-1].start()
        if with_requests:
            own_in.wait()
            ring_in.wait()
            for step in range(steps):
                wide = SIDE // steps

                def one(r, carry):
                    pick_requests(request_group, r, dest_ref, pool_v, given_v)
                    return carry

                lax.fori_loop(step * wide, step * wide + wide, one, 0)
                part = pl.ds(step * wide * SLOTS, wide * SLOTS)
                outs.append(pltpu.make_async_copy(given_v.at[part], given_hbm.at[part], out_sem.at[step]))
                outs[-1].start()
        for out in outs:
            out.wait()

    def piece(count):
        return (count, PIECE, HD)

    shapes, scratch, data = [], [], []
    if with_list:
        shapes.append(jax.ShapeDtypeStruct(piece(2 * CAPS[0]), BF16))
        scratch += [pltpu.VMEM(piece(OWN), BF16), pltpu.VMEM(piece(2 * CAPS[0]), BF16)]
        data.append(own_next)
    if with_requests:
        shapes.append(jax.ShapeDtypeStruct(piece(SIDE * SLOTS), BF16))
        scratch += [pltpu.VMEM(piece(NPIECE), BF16), pltpu.VMEM(piece(SIDE * SLOTS), BF16)]
        data += [own, ring]
    return pl.pallas_call(
        kernel,
        out_shape=tuple(shapes),
        in_specs=[smem, smem] + [hbm] * len(data),
        out_specs=tuple([hbm] * len(shapes)),
        scratch_shapes=scratch + [pltpu.SemaphoreType.DMA((steps + 1,)), pltpu.SemaphoreType.DMA((3,))],
        compiler_params=pltpu.CompilerParams(vmem_limit_bytes=48 << 20),
        name=name,
    )(lists, dest, *data)


def place():
    mem = lax.axis_index("mem")
    plane, me = mem // SIDE, mem % SIDE
    above = ((plane + 1) % PLANES) * SIDE + me
    below = ((plane + PLANES - 1) % PLANES) * SIDE + me
    return plane, me, lax.axis_index("tp"), (above, below)


def greet(ring, partner):
    plane, me, tp, nexts = place()
    barrier = pltpu.get_barrier_semaphore()

    def one(k, carry):
        peer = plane * SIDE + (me + k) % SIDE
        pl.semaphore_signal(barrier, inc=1, device_id=(peer, tp), device_id_type=MESH)
        return carry

    lax.fori_loop(1, SIDE, one, 0)
    count = SIDE - 1
    if ring:
        for peer in nexts:
            pl.semaphore_signal(barrier, inc=1, device_id=(peer, tp), device_id_type=MESH)
        count += 2
    if partner:
        pl.semaphore_signal(
            barrier, inc=1, device_id=(plane * SIDE + me, 1 - tp), device_id_type=MESH
        )
        count += 1
    pl.semaphore_wait(barrier, count)


def spread(g, sources, own, send, recv):
    plane, me, tp, _ = place()
    base = (me // 4) * 128 + (me % 4) * MB

    def parts(i):
        for h in range(HG):
            for kv in range(2):
                yield (
                    sources[kv].at[:, i, :, pl.ds((g * HG + h) * HD, HD)],
                    own.at[pl.ds(base + h * 32, MB), pl.ds(kv * ROWS, ROWS)],
                )

    def to_peer(k, carry):
        i = (me + k) % SIDE
        for source, target in parts(i):
            pltpu.make_async_remote_copy(
                src_ref=source,
                dst_ref=target,
                send_sem=send,
                recv_sem=recv,
                device_id=(plane * SIDE + i, tp),
                device_id_type=MESH,
            ).start()
        return carry

    lax.fori_loop(1, SIDE, to_peer, 0)
    for source, target in parts(me):
        pltpu.make_async_copy(source, target, recv).start()


def spread_wait(own, send, recv):
    pltpu.make_async_copy(own, own, recv).wait()
    sent = own.at[pl.ds(0, (SIDE - 1) * HG * MB)]
    pltpu.make_async_copy(sent, sent, send).wait()


def hop_copy(lst, ring, send, recv, way, part, d):
    _, _, tp, nexts = place()
    low, count = CUTS[part], CUTS[part + 1] - CUTS[part]
    base = way * CSUM + low
    if d == 0:
        source = lst.at[pl.ds(way * CAPS[0] + low, count)]
    else:
        source = ring.at[pl.ds(base + OFFS[d - 1], count)]
    return pltpu.make_async_remote_copy(
        src_ref=source,
        dst_ref=ring.at[pl.ds(base + OFFS[d], count)],
        send_sem=send.at[way, part, d],
        recv_sem=recv.at[way, part, d],
        device_id=(nexts[way], tp),
        device_id_type=MESH,
    )


def hop_first(args):
    for part in range(4):
        for way in range(2):
            hop_copy(*args, way, part, 0).start()


def hop_on(args, d):
    for part in range(4 - d):
        for way in range(2):
            hop_copy(*args, way, part, d - 1).wait_recv()
            hop_copy(*args, way, part, d).start()


def hop_last(args):
    for part in range(4):
        for way in range(2):
            hop_copy(*args, way, part, 3 - part).wait_recv()
            for d in range(4 - part):
                hop_copy(*args, way, part, d).wait_send()


def deliver(given, rcv, send, recv):
    plane, me, tp, _ = place()
    for h in range(HG):

        def to_peer(k, carry):
            i = (me + k) % SIDE
            pltpu.make_async_remote_copy(
                src_ref=given.at[pl.ds(i * SLOTS + h * TOPK, TOPK)],
                dst_ref=rcv.at[h, me],
                send_sem=send,
                recv_sem=recv.at[h],
                device_id=(plane * SIDE + i, tp),
                device_id_type=MESH,
            ).start()
            return carry

        lax.fori_loop(1, SIDE, to_peer, 0)
        pltpu.make_async_copy(
            given.at[pl.ds(me * SLOTS + h * TOPK, TOPK)], rcv.at[h, me], recv.at[h]
        ).start()


def deliver_sent(given, send):
    sent = given.at[pl.ds(0, (SIDE - 1) * SLOTS)]
    pltpu.make_async_copy(sent, sent, send).wait()


def softmax_dot(query, keys, visible):
    scores = dot(query, keys, ((1,), (1,)))
    if visible is not None:
        scores = jnp.where(visible, scores, -1e30)
    highest = jnp.max(scores, axis=1, keepdims=True)
    exponent = jnp.exp2((scores - highest) * SCALE)
    return (exponent * (1.0 / jnp.sum(exponent, axis=1, keepdims=True))).astype(BF16)


def columns(h):
    return pl.ds(pl.multiple_of(h * HD, HD), HD)


def attend_near(g, q_ref, k_ref, v_ref, near):
    def one(h, carry):
        cols = columns(g * HG + h)
        for rb in range(4):
            rows = pl.ds(rb * 128, 128)
            width = (rb + 1) * 128
            visible = iota((128, width), 0) + rb * 128 >= iota((128, width), 1)
            part = softmax_dot(q_ref[rows, cols], k_ref[pl.ds(0, width), cols], visible)
            near[rows, columns(h)] = dot(part, v_ref[pl.ds(0, width), cols], ((1,), (0,)))
        return carry

    lax.fori_loop(0, HG, one, 0)


def attend_far(g, low, high, gate_ref, q_ref, rcv, recv, near, out_ref, done):
    def one(h, carry):
        pltpu.make_async_copy(rcv.at[h], rcv.at[h], recv.at[h]).wait()
        rows = rcv[h].astype(F32).reshape(SIDE * TOPK, PIECE, HD)
        keys = rows[:, :ROWS].reshape(SIDE * TOPK * ROWS, HD).astype(BF16)
        values = rows[:, ROWS:].reshape(SIDE * TOPK * ROWS, HD).astype(BF16)
        cols = columns(g * HG + h)
        gate = gate_ref[g * HG + h]

        def block(rb, inner):
            rows = pl.ds(pl.multiple_of(rb * 128, 128), 128)
            remote = dot(softmax_dot(q_ref[rows, cols], keys, None), values, ((1,), (0,)))
            mixed = gate * remote + (1.0 - gate) * near[rows, columns(h)]
            out_ref[rows, columns(h)] = mixed.astype(BF16)
            return inner

        lax.fori_loop(0, 4, block, 0)
        if done is not None:
            done(h)
        return carry

    lax.fori_loop(low, high, one, 0)


def kernel_spread(
    mem_keys, mem_values, ids_ref, home_ref, own, lists_ref, dest_ref, over_ref, rank_s, address_s, send, recv
):
    plane, _, tp, _ = place()
    greet(False, False)
    spread(0, (mem_keys, mem_values), own, send, recv)
    plan(ids_ref, home_ref, lists_ref, dest_ref, over_ref, rank_s, address_s, plane, tp)
    spread_wait(own, send, recv)


def kernel_ring(mem_keys, mem_values, weight, lst, ring, own_next, other_weight, *sems):
    s1_send, s1_recv, z_send, z_recv, w_sems = sems
    plane, me, tp, _ = place()
    args = (lst, ring, z_send, z_recv)
    greet(True, True)
    hop_first(args)
    spread(1, (mem_keys, mem_values), own_next, s1_send, s1_recv)
    swap = pltpu.make_async_remote_copy(
        src_ref=weight,
        dst_ref=other_weight,
        send_sem=w_sems.at[0],
        recv_sem=w_sems.at[1],
        device_id=(plane * SIDE + me, 1 - tp),
        device_id_type=MESH,
    )
    swap.start()
    for d in range(1, 4):
        hop_on(args, d)
    hop_last(args)
    spread_wait(own_next, s1_send, s1_recv)
    swap.wait()


def kernel_ring_attend(gate_ref, lst, given, q_ref, k_ref, v_ref, ring, out_ref, rcv, near, *sems):
    z_send, z_recv, s3_send, s3_recv = sems
    args = (lst, ring, z_send, z_recv)
    far = (gate_ref, q_ref, rcv, s3_recv, near, out_ref, None)
    greet(True, False)
    hop_first(args)
    deliver(given, rcv, s3_send, s3_recv)
    attend_near(0, q_ref, k_ref, v_ref, near)
    hop_on(args, 1)
    attend_far(0, 0, 2, *far)
    hop_on(args, 2)
    attend_far(0, 2, HG, *far)
    hop_on(args, 3)
    hop_last(args)
    deliver_sent(given, s3_send)


def kernel_attend(
    gate_ref, given, half_ref, weight, other_weight, q_ref, k_ref, v_ref, out_ref,
    rcv, near, half, got, w_own, w_other, total, s3_send, s3_recv, w_sems, half_send, half_recv,
):
    plane, me, tp, _ = place()
    rows = half_ref.shape[0] // 2
    mine = pl.ds(pl.multiple_of(tp * rows, rows), rows)
    theirs = pl.ds(pl.multiple_of((1 - tp) * rows, rows), rows)
    cut = HG * HD

    def swap(source, target, sem):
        return pltpu.make_async_remote_copy(
            src_ref=source,
            dst_ref=target,
            send_sem=half_send.at[sem],
            recv_sem=half_recv.at[sem],
            device_id=(plane * SIDE + me, 1 - tp),
            device_id_type=MESH,
        )

    def head_swap(h):
        return swap(half.at[theirs, columns(h)], got.at[1, :, columns(h)], 1 + h)

    greet(False, True)
    deliver(given, rcv, s3_send, s3_recv)
    first = swap(half_ref.at[theirs], got.at[0], 0)
    first.start()
    loads = [
        pltpu.make_async_copy(weight, w_own, w_sems.at[0]),
        pltpu.make_async_copy(other_weight, w_other, w_sems.at[1]),
    ]
    for load in loads:
        load.start()
    attend_near(1, q_ref, k_ref, v_ref, near)
    for load in loads:
        load.wait()
    first.wait()

    def early(n, carry):
        cols = pl.ds(pl.multiple_of(n * 256, 256), 256)
        total[:, cols] = dot(half_ref[mine], w_own[:cut, cols], ((1,), (0,))) + dot(
            got[0], w_other[:cut, cols], ((1,), (0,))
        )
        return carry

    lax.fori_loop(0, out_ref.shape[1] // 256, early, 0)
    attend_far(
        1, 0, HG, gate_ref, q_ref, rcv, s3_recv, near, half, lambda h: head_swap(h).start()
    )
    for h in range(HG):
        head_swap(h).wait()

    def late(n, carry):
        cols = pl.ds(pl.multiple_of(n * 256, 256), 256)
        mixed = total[:, cols] + dot(half[mine], w_own[cut:, cols], ((1,), (0,)))
        mixed = mixed + dot(got[1], w_other[cut:, cols], ((1,), (0,)))
        out_ref[:, cols] = mixed.astype(BF16)
        return carry

    lax.fori_loop(0, out_ref.shape[1] // 256, late, 0)
    deliver_sent(given, s3_send)


SMEM = pl.BlockSpec(memory_space=pltpu.SMEM)
HBM = pl.BlockSpec(memory_space=pl.ANY)
VMEM = pl.BlockSpec(memory_space=pltpu.VMEM)


def call(kernel, name, number, outs, in_specs, out_specs, scratch, *args):
    return pl.pallas_call(
        kernel,
        out_shape=outs,
        in_specs=in_specs,
        out_specs=out_specs,
        scratch_shapes=scratch,
        compiler_params=pltpu.CompilerParams(
            collective_id=number, has_side_effects=True, vmem_limit_bytes=48 << 20
        ),
        name=name,
    )(*args)


def shape(dims, dtype=BF16):
    return jax.ShapeDtypeStruct(dims, dtype)


def view(rows):
    return rows.reshape(MB, SIDE, ROWS, HL * HD)


def start(mem_keys, mem_values, block_ids, block_home):
    ids = block_ids.transpose(1, 2, 0).reshape(2, HL, TOPK, PLANES * SIDE)
    one = pltpu.SemaphoreType.DMA
    return call(
        kernel_spread, "spread", 0,
        (
            shape((OWN, PIECE, HD)), shape((4, LPAD), jnp.int32),
            shape((HL * TOPK, PLANES * SIDE), jnp.int32), shape((8, 128), F32),
        ),
        [HBM, HBM, VMEM, VMEM], (HBM, VMEM, VMEM, VMEM),
        [pltpu.VMEM((2, PLANES, 4, 256), jnp.int32), pltpu.VMEM((HL, 64, 32), F32), one, one],
        view(mem_keys), view(mem_values), ids, block_home.reshape(8, 128),
    )


def fast_path(own0, lists, dest, gate, mem_keys, mem_values, queries, local_keys, local_values, out_weight):
    tokens = queries.shape[0]
    half = (tokens, HG * HD)
    ring_shape = shape((2 * CSUM, PIECE, HD))
    one = pltpu.SemaphoreType.DMA
    pair, heads, ring = one((2,)), one((HG,)), one((2, 4, 4))
    swaps = one((HG + 1,))
    rcv = pltpu.VMEM((HG, SIDE, TOPK, PIECE, HD), BF16)
    near = pltpu.VMEM(half, F32)
    (lst0,) = pick("pick_first", 0, None, lists, dest, own0, None, None)
    ring0, own1, other_weight = call(
        kernel_ring, "ring", 1, (ring_shape, shape(own0.shape), shape(out_weight.shape)),
        [HBM] * 4, (HBM, HBM, HBM), [one, one, ring, ring, pair],
        view(mem_keys), view(mem_values), out_weight, lst0,
    )
    lst1, given0 = pick("pick_both", 1, 0, lists, dest, own1, own0, ring0)
    ring1, half0 = call(
        kernel_ring_attend, "ring_attend", 2, (ring_shape, shape(half)),
        [SMEM, HBM, HBM, VMEM, VMEM, VMEM], (HBM, VMEM), [rcv, near, ring, ring, one, heads],
        gate, lst1, given0, queries, local_keys, local_values,
    )
    (given1,) = pick("pick_last", None, 1, lists, dest, None, own1, ring1)
    weight = pltpu.VMEM(out_weight.shape, BF16)
    return call(
        kernel_attend, "attend", 3, shape((tokens // 2, out_weight.shape[1])),
        [SMEM, HBM, VMEM, HBM, HBM, VMEM, VMEM, VMEM], VMEM,
        [
            rcv, near, pltpu.VMEM(half, BF16), pltpu.VMEM((2, tokens // 2, HG * HD), BF16),
            weight, weight, pltpu.VMEM((tokens // 2, out_weight.shape[1]), F32),
            one, heads, pair, swaps, swaps,
        ],
        gate, given1, half0, out_weight, other_weight, queries, local_keys, local_values,
    )


def rank_within(owner_row):
    request_count = owner_row.shape[0]
    order_index = jnp.arange(request_count, dtype=jnp.int32)
    earlier = order_index[:, None] > order_index[None, :]
    same_owner = owner_row[:, None] == owner_row[None, :]
    return jnp.sum((same_owner & earlier).astype(jnp.int32), axis=1)


def slow_path(
    gate, mem_keys, mem_values, queries, local_keys, local_values, out_weight, block_ids, block_home
):
    mem_count = lax.axis_size("mem")
    mem_index = lax.axis_index("mem")
    tp_index = lax.axis_index("tp")
    requests = HL * TOPK
    slots = 2
    group_ids = lax.dynamic_slice_in_dim(block_ids, tp_index * HL, HL, 1).reshape(mem_count, requests)
    home_slots = jnp.take(block_home, group_ids, axis=0)
    owners = home_slots // MB
    codes = (home_slots % MB) * HL + jnp.arange(requests, dtype=jnp.int32)[None, :] // TOPK
    own_owners = lax.dynamic_index_in_dim(owners, mem_index, 0, keepdims=False)
    own_codes = lax.dynamic_index_in_dim(codes, mem_index, 0, keepdims=False)
    own_ranks = rank_within(own_owners)
    slot_index = jnp.arange(slots, dtype=jnp.int32)
    owner_index = jnp.arange(mem_count, dtype=jnp.int32)
    matches = (own_owners[None, None, :] == owner_index[:, None, None]) & (
        own_ranks[None, None, :] == slot_index[None, :, None]
    )
    table = jnp.sum(jnp.where(matches, own_codes[None, None, :], 0), axis=2)
    wanted = lax.all_to_all(table, "mem", split_axis=0, concat_axis=0, tiled=True)
    flat_slot = own_owners * slots + own_ranks

    def fetch(rows):
        blocks = rows.reshape(MB, BLK, HL, HD)
        sent = blocks[wanted // HL, :, wanted % HL, :]
        got = lax.all_to_all(sent, "mem", split_axis=0, concat_axis=0, tiled=True)
        far = jnp.take(got.reshape(mem_count * slots, BLK, HD), flat_slot, axis=0)
        return far.reshape(HL, TOPK * BLK, HD)

    positions = jnp.arange(queries.shape[0], dtype=jnp.int32)
    causal = positions[:, None] >= positions[None, :]

    def by_head(x):
        return x.reshape(x.shape[0], HL, HD).transpose(1, 0, 2)

    def one_head(parts):
        q, far_k, far_v, near_k, near_v, g = parts
        remote = dot(softmax_dot(q, far_k, None), far_v, ((1,), (0,)))
        nearby = dot(softmax_dot(q, near_k, causal), near_v, ((1,), (0,)))
        return (g * remote + (1.0 - g) * nearby).astype(BF16)

    out = lax.map(
        one_head,
        (by_head(queries), fetch(mem_keys), fetch(mem_values), by_head(local_keys), by_head(local_values), gate),
    )
    combined = out.transpose(1, 0, 2).reshape(queries.shape)
    partial = jnp.dot(combined, out_weight, preferred_element_type=F32)
    return lax.psum_scatter(partial, "tp", scatter_dimension=0, tiled=True).astype(BF16)


def per_device(
    queries, local_keys, local_values, mem_keys, mem_values, gate_bias, out_weight, block_ids, block_home
):
    gate = jax.nn.sigmoid(gate_bias)
    own0, lists, dest, over = start(mem_keys, mem_values, block_ids, block_home)
    attention = (gate, mem_keys, mem_values, queries, local_keys, local_values, out_weight)
    return lax.cond(
        over[0, 0] <= 0.5,
        lambda: fast_path(own0, lists, dest, *attention),
        lambda: slow_path(*attention, block_ids, block_home),
    )


def solution(mesh):
    in_specs = (
        P("mem", "tp"), P("mem", "tp"), P("mem", "tp"), P("mem", "tp"), P("mem", "tp"),
        P("tp"), P("tp", None), P(), P(),
    )
    return jax.shard_map(
        per_device, mesh=mesh, in_specs=in_specs, out_specs=P(("mem", "tp"), None), check_vma=False
    )
```

```python
import functools
import math

import jax
import jax.numpy as jnp
from jax import lax
from jax.experimental import pallas as pl
from jax.experimental.pallas import tpu as pltpu
from jax.sharding import PartitionSpec as P

HD = 128
BLK = 128
TOPK = 16
PLANES = 8
SIDE = 16
HL = 8
GROUPS = 2
HG = HL // GROUPS
MB = 8
ROWS = BLK // SIDE
OWN = SIDE * MB * HG
CAPS = (344, 280, 200, 88)
OFFS = (0, 344, 624, 824)
CSUM = 912
CUTS = (0, 88, 200, 280, 344)
NPIECE = OWN + 2 * CSUM
PIECE = 2 * ROWS
LPAD = 384
SLOTS = HG * TOPK
MESH = pl.DeviceIdType.MESH
F32 = jnp.float32
BF16 = jnp.bfloat16
SCALE = math.log2(math.e) / math.sqrt(HD)


def iota(shape, axis):
    return lax.broadcasted_iota(jnp.int32, shape, axis)


def hot(mask):
    return jnp.where(mask, 1.0, 0.0).astype(BF16)


def dot(a, b, dims):
    return lax.dot_general(a, b, (dims, ((), ())), preferred_element_type=F32)


def ways(dz, even):
    up = ((dz >= 1) & (dz <= 3)) | ((dz == 4) & even)
    down = (dz >= 5) | ((dz == 4) & jnp.logical_not(even))
    return up, down


def find(ids_ref, home_ref, side, h):
    home = home_ref[...]
    home = jnp.concatenate([home >> 5, home & 31], axis=0).astype(F32).astype(BF16)
    block = ids_ref[side, h]
    ids = jnp.concatenate([block[q : q + 1] for q in range(TOPK)], axis=1)
    both = dot(home, hot(iota((128, 2048), 0) == (ids & 127)), ((1,), (0,)))
    at_hi = iota((8, 2048), 0) == (ids >> 7)
    pos_hi = jnp.sum(jnp.where(at_hi, both[:8], 0.0), axis=0, keepdims=True).astype(jnp.int32)
    pos_lo = jnp.sum(jnp.where(at_hi, both[8:], 0.0), axis=0, keepdims=True).astype(jnp.int32)
    return hot(iota((32, 2048), 0) == pos_hi), pos_lo


def plan_requests(ids_ref, home_ref, address_ref, dest_ref, tp):
    def one_dest(h, carry):
        by_hi, pos_lo = find(ids_ref, home_ref, tp, h)
        found = dot(address_ref[h].astype(BF16), by_hi, ((1,), (0,)))
        at_lo = iota((32, 2048), 0) == pos_lo
        dest_hi = jnp.sum(jnp.where(at_lo, found[:32], 0.0), axis=0, keepdims=True)
        dest_lo = jnp.sum(jnp.where(at_lo, found[32:], 0.0), axis=0, keepdims=True)
        dest = (dest_hi * 32.0 + dest_lo).astype(jnp.int32)
        rows = jnp.concatenate([dest[:, q * 128 : q * 128 + 128] for q in range(TOPK)], axis=0)
        dest_ref[pl.ds(pl.multiple_of(h * TOPK, TOPK), TOPK), :] = rows
        return carry

    lax.fori_loop(0, HL, one_dest, 0)


def plan_ring(ids_ref, home_ref, lists_ref, address_ref, over_ref, rank_s, plane, tp):
    lane = iota((1, 2048), 1)
    plane_term = ((lane & 127) >> 4) * 32
    row_plane = iota((32, 256), 0) >> 2
    even = (iota((32, 256), 1) & 1) == 0
    dz = ((iota((32, 256), 1) >> 5) - row_plane) & 7
    up, down = ways(dz, even)
    reach = (jnp.where(up, dz, 0), jnp.where(down, 8 - dz, 0))

    r, s = iota((256, 256), 0), iota((256, 256), 1)
    same_group = (r >> 7) == (s >> 7)
    prefix = hot(same_group & (r <= s))
    whole = hot(same_group)
    same_plane = (r >> 2) == (s >> 2)
    rows_before = hot(same_plane & (s < r))
    rows_all = hot(same_plane)
    over = jnp.zeros((32, 256), F32)
    ranks = []
    for other in range(2):
        side = tp if other == 0 else 1 - tp

        def one_head(h, far):
            by_hi, pos_lo = find(ids_ref, home_ref, side, h)
            count = dot(by_hi, hot(iota((256, 2048), 0) == plane_term + pos_lo), ((1,), (1,)))
            out = []
            for way in range(2):
                value = jnp.where(count > 0.5, reach[way], 0)
                for shift in (128, 64, 32):
                    value = jnp.maximum(value, pltpu.roll(value, shift, 1))
                out.append(jnp.where((iota((32, 256), 1) >> 5) == h, value, far[way]))
            return tuple(out)

        zero = jnp.zeros((32, 256), jnp.int32)
        far = lax.fori_loop(0, HL, one_head, (zero, zero))
        levels = jnp.concatenate(
            [jnp.where(far[way] == d, 1.0, 0.0) for way in range(2) for d in (4, 3, 2, 1)], axis=0
        )
        level_hot = levels.astype(BF16)
        before_lane = dot(level_hot, prefix, ((1,), (0,)))
        row_total = dot(level_hot, whole, ((1,), (0,))).astype(BF16)
        before_row = dot(rows_before, row_total, ((1,), (0,)))
        plane_total = dot(rows_all, row_total, ((1,), (0,)))
        for way in range(2):
            base = jnp.zeros((32, 256), F32)
            rank = jnp.zeros((32, 256), F32)
            for e in range(4):
                part = slice((way * 4 + e) * 32, (way * 4 + e) * 32 + 32)
                rank = rank + levels[part] * (base + before_row[part] + before_lane[part])
                base = base + plane_total[part]
                over = jnp.maximum(over, base - float(CAPS[3 - e]))
            if other == 0:
                ranks.append(rank.astype(jnp.int32) - 1)
                for p in range(PLANES):
                    rank_s[way, p] = ranks[way][p * 4 : p * 4 + 4]
    over_ref[...] = jnp.broadcast_to(jnp.max(over, keepdims=True), (8, 128))

    values = jnp.where(iota((8, 128), 0) == 0, iota((8, 128), 1), 1).astype(F32).astype(BF16)
    for way in range(2):
        mine = rank_s[way, plane]
        for g in range(GROUPS):
            index = jnp.zeros((1, LPAD), F32)
            for rr in range(4):
                wanted = mine[rr : rr + 1, g * 128 : g * 128 + 128]
                got = dot(values, hot(iota((LPAD, 128), 0) == wanted), ((1,), (1,)))
                index = index + got[0:1] + got[1:2] * float(rr * 128)
            lists_ref[g * 2 + way : g * 2 + way + 1, :] = index.astype(jnp.int32)

    dz = (plane - row_plane) & 7
    up, down = ways(dz, even)
    address = (iota((32, 256), 0) & 3) * 128 + (iota((32, 256), 1) & 127)
    for d in range(1, 5):
        address = jnp.where(up & (dz == d), ranks[0] + (OWN + OFFS[d - 1]), address)
        address = jnp.where(down & (8 - dz == d), ranks[1] + (OWN + CSUM + OFFS[d - 1]), address)
    high = jnp.transpose((address >> 5).astype(F32))
    low = jnp.transpose((address & 31).astype(F32))
    for h in range(HL):
        part = slice(h * 32, h * 32 + 32)
        address_ref[h] = jnp.concatenate([high[part], low[part]], axis=0)


def pick_list(g, lists_ref, own, out):
    for way in range(2):

        def one(j, carry):
            out[way * CAPS[0] + j] = own[lists_ref[g * 2 + way, j]]
            return carry

        lax.fori_loop(0, CAPS[0], one, 0, unroll=43)


def pick_requests(g, r, dest_ref, pool, out):
    column = (lax.axis_index("mem") // SIDE) * SIDE + r

    for j in range(SLOTS):
        out[r * SLOTS + j] = pool[dest_ref[g * SLOTS + j, column]]


def pick(name, list_group, request_group, lists, dest, own_next, own, ring):
    smem = pl.BlockSpec(memory_space=pltpu.SMEM)
    hbm = pl.BlockSpec(memory_space=pl.ANY)
    with_list, with_requests = own_next is not None, own is not None
    steps = 4

    def kernel(*refs):
        refs = list(refs)
        lists_ref, dest_ref = refs.pop(0), refs.pop(0)
        next_hbm = refs.pop(0) if with_list else None
        own_hbm, ring_hbm = (refs.pop(0), refs.pop(0)) if with_requests else (None, None)
        list_hbm = refs.pop(0) if with_list else None
        given_hbm = refs.pop(0) if with_requests else None
        out_sem, in_sem = refs.pop(), refs.pop()
        if with_list:
            next_v, list_v = refs.pop(0), refs.pop(0)
            next_in = pltpu.make_async_copy(next_hbm, next_v, in_sem.at[0])
            next_in.start()
        if with_requests:
            pool_v, given_v = refs.pop(0), refs.pop(0)
            own_in = pltpu.make_async_copy(own_hbm, pool_v.at[pl.ds(0, OWN)], in_sem.at[1])
            cut = CSUM // 2
            ring_in = [
                pltpu.make_async_copy(
                    ring_hbm.at[pl.ds(n * cut, cut)], pool_v.at[pl.ds(OWN + n * cut, cut)], in_sem.at[2 + n]
                )
                for n in range(4)
            ]
            for copy in ring_in + [own_in]:
                copy.start()
        outs = []
        if with_list:
            next_in.wait()
            pick_list(list_group, lists_ref, next_v, list_v)
            outs.append(pltpu.make_async_copy(list_v, list_hbm, out_sem.at[steps]))
            outs[-1].start()
        if with_requests:
            for copy in ring_in + [own_in]:
                copy.wait()
            for step in range(steps):
                wide = SIDE // steps

                def one(r, carry):
                    pick_requests(request_group, r, dest_ref, pool_v, given_v)
                    return carry

                lax.fori_loop(step * wide, step * wide + wide, one, 0)
                part = pl.ds(step * wide * SLOTS, wide * SLOTS)
                outs.append(pltpu.make_async_copy(given_v.at[part], given_hbm.at[part], out_sem.at[step]))
                outs[-1].start()
        for out in outs:
            out.wait()

    def piece(count):
        return (count, PIECE, HD)

    shapes, scratch, data = [], [], []
    if with_list:
        shapes.append(jax.ShapeDtypeStruct(piece(2 * CAPS[0]), BF16))
        scratch += [pltpu.VMEM(piece(OWN), BF16), pltpu.VMEM(piece(2 * CAPS[0]), BF16)]
        data.append(own_next)
    if with_requests:
        shapes.append(jax.ShapeDtypeStruct(piece(SIDE * SLOTS), BF16))
        scratch += [pltpu.VMEM(piece(NPIECE), BF16), pltpu.VMEM(piece(SIDE * SLOTS), BF16)]
        data += [own, ring]
    return pl.pallas_call(
        kernel,
        out_shape=tuple(shapes),
        in_specs=[smem, smem] + [hbm] * len(data),
        out_specs=tuple([hbm] * len(shapes)),
        scratch_shapes=scratch + [pltpu.SemaphoreType.DMA((6,)), pltpu.SemaphoreType.DMA((steps + 1,))],
        compiler_params=pltpu.CompilerParams(vmem_limit_bytes=(24 if with_requests else 10) << 20),
        name=name,
    )(lists, dest, *data)


def place():
    mem = lax.axis_index("mem")
    plane, me = mem // SIDE, mem % SIDE
    above = ((plane + 1) % PLANES) * SIDE + me
    below = ((plane + PLANES - 1) % PLANES) * SIDE + me
    return plane, me, lax.axis_index("tp"), (above, below)


def peer_of(me, k):
    step = (k * 7) % SIDE
    return ((me // 4 + step // 4) % 4) * 4 + (me % 4 + step % 4) % 4


def greet(ring, partner):
    plane, me, tp, nexts = place()
    barrier = pltpu.get_barrier_semaphore()

    def one(k, carry):
        peer = plane * SIDE + peer_of(me, k)
        pl.semaphore_signal(barrier, inc=1, device_id=(peer, tp), device_id_type=MESH)
        return carry

    lax.fori_loop(1, SIDE, one, 0)
    count = SIDE - 1
    if ring:
        for peer in nexts:
            pl.semaphore_signal(barrier, inc=1, device_id=(peer, tp), device_id_type=MESH)
        count += 2
    if partner:
        pl.semaphore_signal(
            barrier, inc=1, device_id=(plane * SIDE + me, 1 - tp), device_id_type=MESH
        )
        count += 1
    pl.semaphore_wait(barrier, count)


def spread(g, sources, own, send, recv):
    plane, me, tp, _ = place()
    base = (me // 4) * 128 + (me % 4) * MB

    def parts(i):
        for h in range(HG):
            for kv in range(2):
                yield (
                    sources[kv].at[:, i, :, pl.ds((g * HG + h) * HD, HD)],
                    own.at[pl.ds(base + h * 32, MB), pl.ds(kv * ROWS, ROWS)],
                )

    def to_peer(k, carry):
        i = peer_of(me, k)
        for source, target in parts(i):
            pltpu.make_async_remote_copy(
                src_ref=source,
                dst_ref=target,
                send_sem=send,
                recv_sem=recv,
                device_id=(plane * SIDE + i, tp),
                device_id_type=MESH,
            ).start()
        return carry

    lax.fori_loop(1, SIDE, to_peer, 0)
    for source, target in parts(me):
        pltpu.make_async_copy(source, target, recv).start()


def spread_wait(own, send, recv):
    pltpu.make_async_copy(own, own, recv).wait()
    sent = own.at[pl.ds(0, (SIDE - 1) * HG * MB)]
    pltpu.make_async_copy(sent, sent, send).wait()


def hop_copy(lst, ring, send, recv, way, part, d):
    _, _, tp, nexts = place()
    low, count = CUTS[part], CUTS[part + 1] - CUTS[part]
    base = way * CSUM + low
    if d == 0:
        source = lst.at[pl.ds(way * CAPS[0] + low, count)]
    else:
        source = ring.at[pl.ds(base + OFFS[d - 1], count)]
    return pltpu.make_async_remote_copy(
        src_ref=source,
        dst_ref=ring.at[pl.ds(base + OFFS[d], count)],
        send_sem=send.at[way, part, d],
        recv_sem=recv.at[way, part, d],
        device_id=(nexts[way], tp),
        device_id_type=MESH,
    )


def hop_first(args):
    for part in range(4):
        for way in range(2):
            hop_copy(*args, way, part, 0).start()


def hop_on(args, d):
    for part in range(4 - d):
        for way in range(2):
            hop_copy(*args, way, part, d - 1).wait_recv()
            hop_copy(*args, way, part, d).start()


def hop_last(args):
    for part in range(4):
        for way in range(2):
            hop_copy(*args, way, part, 3 - part).wait_recv()
            for d in range(4 - part):
                hop_copy(*args, way, part, d).wait_send()


def deliver(given, rcv, send, recv):
    plane, me, tp, _ = place()
    for h in range(HG):

        def to_peer(k, carry):
            i = peer_of(me, k)
            pltpu.make_async_remote_copy(
                src_ref=given.at[pl.ds(i * SLOTS + h * TOPK, TOPK)],
                dst_ref=rcv.at[h, me],
                send_sem=send,
                recv_sem=recv.at[h],
                device_id=(plane * SIDE + i, tp),
                device_id_type=MESH,
            ).start()
            return carry

        lax.fori_loop(1, SIDE, to_peer, 0)
        pltpu.make_async_copy(
            given.at[pl.ds(me * SLOTS + h * TOPK, TOPK)], rcv.at[h, me], recv.at[h]
        ).start()


def deliver_sent(given, send):
    sent = given.at[pl.ds(0, (SIDE - 1) * SLOTS)]
    pltpu.make_async_copy(sent, sent, send).wait()


def softmax_dot(query, keys, visible):
    scores = dot(query, keys, ((1,), (1,)))
    if visible is not None:
        scores = jnp.where(visible, scores, -1e30)
    highest = jnp.max(scores, axis=1, keepdims=True)
    exponent = jnp.exp2((scores - highest) * SCALE)
    return (exponent * (1.0 / jnp.sum(exponent, axis=1, keepdims=True))).astype(BF16)


def columns(h):
    return pl.ds(pl.multiple_of(h * HD, HD), HD)


def attend_near(g, q_ref, k_ref, v_ref, near):
    def one(h, carry):
        cols = columns(g * HG + h)
        for rb in range(4):
            rows = pl.ds(rb * 128, 128)
            width = (rb + 1) * 128
            visible = iota((128, width), 0) + rb * 128 >= iota((128, width), 1)
            part = softmax_dot(q_ref[rows, cols], k_ref[pl.ds(0, width), cols], visible)
            near[rows, columns(h)] = dot(part, v_ref[pl.ds(0, width), cols], ((1,), (0,)))
        return carry

    lax.fori_loop(0, HG, one, 0)


def attend_far(g, low, high, gate_ref, q_ref, rcv, recv, near, out_ref, done):
    def one(h, carry):
        pltpu.make_async_copy(rcv.at[h], rcv.at[h], recv.at[h]).wait()
        rows = rcv[h].astype(F32).reshape(SIDE * TOPK, PIECE, HD)
        keys = rows[:, :ROWS].reshape(SIDE * TOPK * ROWS, HD).astype(BF16)
        values = rows[:, ROWS:].reshape(SIDE * TOPK * ROWS, HD).astype(BF16)
        cols = columns(g * HG + h)
        gate = gate_ref[g * HG + h]

        def block(rb, inner):
            rows = pl.ds(pl.multiple_of(rb * 128, 128), 128)
            remote = dot(softmax_dot(q_ref[rows, cols], keys, None), values, ((1,), (0,)))
            mixed = gate * remote + (1.0 - gate) * near[rows, columns(h)]
            out_ref[rows, columns(h)] = mixed.astype(BF16)
            return inner

        lax.fori_loop(0, 4, block, 0)
        if done is not None:
            done(h)
        return carry

    lax.fori_loop(low, high, one, 0)


def kernel_spread(
    mem_keys, mem_values, ids_ref, home_ref, own, lists_ref, address_ref, over_ref, rank_s, send, recv
):
    plane, _, tp, _ = place()
    greet(False, False)
    spread(0, (mem_keys, mem_values), own, send, recv)
    plan_ring(ids_ref, home_ref, lists_ref, address_ref, over_ref, rank_s, plane, tp)
    spread_wait(own, send, recv)


def kernel_ring(
    mem_keys, mem_values, lst, ids_ref, home_ref, address_ref, ring, own_next, dest_ref, *sems
):
    s1_send, s1_recv, z_send, z_recv = sems
    args = (lst, ring, z_send, z_recv)
    greet(True, False)
    hop_first(args)
    spread(1, (mem_keys, mem_values), own_next, s1_send, s1_recv)
    for d in range(1, 4):
        hop_on(args, d)
    plan_requests(ids_ref, home_ref, address_ref, dest_ref, lax.axis_index("tp"))
    hop_last(args)
    spread_wait(own_next, s1_send, s1_recv)


def kernel_ring_attend(
    gate_ref, lst, given, weight, q_ref, k_ref, v_ref, ring, out_ref, other_weight, rcv, near, *sems
):
    z_send, z_recv, s3_send, s3_recv, w_sems = sems
    plane, me, tp, _ = place()
    args = (lst, ring, z_send, z_recv)
    far = (gate_ref, q_ref, rcv, s3_recv, near, out_ref, None)
    greet(True, True)
    hop_first(args)
    deliver(given, rcv, s3_send, s3_recv)
    swap = pltpu.make_async_remote_copy(
        src_ref=weight,
        dst_ref=other_weight,
        send_sem=w_sems.at[0],
        recv_sem=w_sems.at[1],
        device_id=(plane * SIDE + me, 1 - tp),
        device_id_type=MESH,
    )
    swap.start()
    attend_near(0, q_ref, k_ref, v_ref, near)
    hop_on(args, 1)
    attend_far(0, 0, 2, *far)
    hop_on(args, 2)
    attend_far(0, 2, HG, *far)
    hop_on(args, 3)
    hop_last(args)
    deliver_sent(given, s3_send)
    swap.wait()


def kernel_attend(
    gate_ref, given, half_ref, weight, other_weight, q_ref, k_ref, v_ref, out_ref,
    rcv, near, half, got, w_own, w_other, total, s3_send, s3_recv, w_sems, half_send, half_recv,
):
    plane, me, tp, _ = place()
    rows = half_ref.shape[0] // 2
    mine = pl.ds(pl.multiple_of(tp * rows, rows), rows)
    theirs = pl.ds(pl.multiple_of((1 - tp) * rows, rows), rows)
    cut = HG * HD

    def swap(source, target, sem):
        return pltpu.make_async_remote_copy(
            src_ref=source,
            dst_ref=target,
            send_sem=half_send.at[sem],
            recv_sem=half_recv.at[sem],
            device_id=(plane * SIDE + me, 1 - tp),
            device_id_type=MESH,
        )

    def head_swap(h):
        return swap(half.at[theirs, columns(h)], got.at[1, :, columns(h)], 1 + h)

    greet(False, True)
    deliver(given, rcv, s3_send, s3_recv)
    first = swap(half_ref.at[theirs], got.at[0], 0)
    first.start()
    loads = [
        pltpu.make_async_copy(weight, w_own, w_sems.at[0]),
        pltpu.make_async_copy(other_weight, w_other, w_sems.at[1]),
    ]
    for load in loads:
        load.start()
    attend_near(1, q_ref, k_ref, v_ref, near)
    for load in loads:
        load.wait()
    first.wait()

    def early(n, carry):
        cols = pl.ds(pl.multiple_of(n * 256, 256), 256)
        total[:, cols] = dot(half_ref[mine], w_own[:cut, cols], ((1,), (0,))) + dot(
            got[0], w_other[:cut, cols], ((1,), (0,))
        )
        return carry

    lax.fori_loop(0, out_ref.shape[1] // 256, early, 0)
    attend_far(
        1, 0, HG, gate_ref, q_ref, rcv, s3_recv, near, half, lambda h: head_swap(h).start()
    )
    for h in range(HG):
        head_swap(h).wait()

    def late(n, carry):
        cols = pl.ds(pl.multiple_of(n * 256, 256), 256)
        mixed = total[:, cols] + dot(half[mine], w_own[cut:, cols], ((1,), (0,)))
        mixed = mixed + dot(got[1], w_other[cut:, cols], ((1,), (0,)))
        out_ref[:, cols] = mixed.astype(BF16)
        return carry

    lax.fori_loop(0, out_ref.shape[1] // 256, late, 0)
    deliver_sent(given, s3_send)


SMEM = pl.BlockSpec(memory_space=pltpu.SMEM)
HBM = pl.BlockSpec(memory_space=pl.ANY)
VMEM = pl.BlockSpec(memory_space=pltpu.VMEM)


def call(kernel, name, number, mib, outs, in_specs, out_specs, scratch, *args):
    return pl.pallas_call(
        kernel,
        out_shape=outs,
        in_specs=in_specs,
        out_specs=out_specs,
        scratch_shapes=scratch,
        compiler_params=pltpu.CompilerParams(
            collective_id=number, has_side_effects=True, vmem_limit_bytes=mib << 20
        ),
        name=name,
    )(*args)


def shape(dims, dtype=BF16):
    return jax.ShapeDtypeStruct(dims, dtype)


def view(rows):
    return rows.reshape(MB, SIDE, ROWS, HL * HD)


def start(mem_keys, mem_values, ids, home):
    one = pltpu.SemaphoreType.DMA
    return call(
        kernel_spread, "spread", 0, 24,
        (
            shape((OWN, PIECE, HD)), shape((4, LPAD), jnp.int32),
            shape((HL, 64, 32), F32), shape((8, 128), F32),
        ),
        [HBM, HBM, VMEM, VMEM], (HBM, VMEM, VMEM, VMEM),
        [pltpu.VMEM((2, PLANES, 4, 256), jnp.int32), one, one],
        view(mem_keys), view(mem_values), ids, home,
    )


def fast_path(
    own0, lists, address, ids, home, gate,
    mem_keys, mem_values, queries, local_keys, local_values, out_weight,
):
    tokens = queries.shape[0]
    half = (tokens, HG * HD)
    ring_shape = shape((2 * CSUM, PIECE, HD))
    one = pltpu.SemaphoreType.DMA
    pair, heads, ring = one((2,)), one((HG,)), one((2, 4, 4))
    swaps = one((HG + 1,))
    rcv = pltpu.VMEM((HG, SIDE, TOPK, PIECE, HD), BF16)
    near = pltpu.VMEM(half, F32)
    (lst0,) = pick("pick_first", 0, None, lists, lists, own0, None, None)
    ring0, own1, dest = call(
        kernel_ring, "ring", 1, 16,
        (ring_shape, shape(own0.shape), shape((HL * TOPK, PLANES * SIDE), jnp.int32)),
        [HBM, HBM, HBM, VMEM, VMEM, VMEM], (HBM, HBM, VMEM), [one, one, ring, ring],
        view(mem_keys), view(mem_values), lst0, ids, home, address,
    )
    lst1, given0 = pick("pick_both", 1, 0, lists, dest, own1, own0, ring0)
    ring1, half0, other_weight = call(
        kernel_ring_attend, "ring_attend", 2, 28,
        (ring_shape, shape(half), shape(out_weight.shape)),
        [SMEM, HBM, HBM, HBM, VMEM, VMEM, VMEM], (HBM, VMEM, HBM),
        [rcv, near, ring, ring, one, heads, pair],
        gate, lst1, given0, out_weight, queries, local_keys, local_values,
    )
    (given1,) = pick("pick_last", None, 1, lists, dest, None, own1, ring1)
    weight = pltpu.VMEM(out_weight.shape, BF16)
    return call(
        kernel_attend, "attend", 3, 40, shape((tokens // 2, out_weight.shape[1])),
        [SMEM, HBM, VMEM, HBM, HBM, VMEM, VMEM, VMEM], VMEM,
        [
            rcv, near, pltpu.VMEM(half, BF16), pltpu.VMEM((2, tokens // 2, HG * HD), BF16),
            weight, weight, pltpu.VMEM((tokens // 2, out_weight.shape[1]), F32),
            one, heads, pair, swaps, swaps,
        ],
        gate, given1, half0, out_weight, other_weight, queries, local_keys, local_values,
    )


def rank_within(owner_row):
    request_count = owner_row.shape[0]
    order_index = jnp.arange(request_count, dtype=jnp.int32)
    earlier = order_index[:, None] > order_index[None, :]
    same_owner = owner_row[:, None] == owner_row[None, :]
    return jnp.sum((same_owner & earlier).astype(jnp.int32), axis=1)


def slow_path(
    gate, mem_keys, mem_values, queries, local_keys, local_values, out_weight, block_ids, block_home
):
    mem_count = lax.axis_size("mem")
    mem_index = lax.axis_index("mem")
    tp_index = lax.axis_index("tp")
    requests = HL * TOPK
    slots = 2
    group_ids = lax.dynamic_slice_in_dim(block_ids, tp_index * HL, HL, 1).reshape(mem_count, requests)
    home_slots = jnp.take(block_home, group_ids, axis=0)
    owners = home_slots // MB
    codes = (home_slots % MB) * HL + jnp.arange(requests, dtype=jnp.int32)[None, :] // TOPK
    own_owners = lax.dynamic_index_in_dim(owners, mem_index, 0, keepdims=False)
    own_codes = lax.dynamic_index_in_dim(codes, mem_index, 0, keepdims=False)
    own_ranks = rank_within(own_owners)
    slot_index = jnp.arange(slots, dtype=jnp.int32)
    owner_index = jnp.arange(mem_count, dtype=jnp.int32)
    matches = (own_owners[None, None, :] == owner_index[:, None, None]) & (
        own_ranks[None, None, :] == slot_index[None, :, None]
    )
    table = jnp.sum(jnp.where(matches, own_codes[None, None, :], 0), axis=2)
    wanted = lax.all_to_all(table, "mem", split_axis=0, concat_axis=0, tiled=True)
    flat_slot = own_owners * slots + own_ranks

    def fetch(rows):
        blocks = rows.reshape(MB, BLK, HL, HD)
        sent = blocks[wanted // HL, :, wanted % HL, :]
        got = lax.all_to_all(sent, "mem", split_axis=0, concat_axis=0, tiled=True)
        far = jnp.take(got.reshape(mem_count * slots, BLK, HD), flat_slot, axis=0)
        return far.reshape(HL, TOPK * BLK, HD)

    positions = jnp.arange(queries.shape[0], dtype=jnp.int32)
    causal = positions[:, None] >= positions[None, :]

    def by_head(x):
        return x.reshape(x.shape[0], HL, HD).transpose(1, 0, 2)

    def one_head(parts):
        q, far_k, far_v, near_k, near_v, g = parts
        remote = dot(softmax_dot(q, far_k, None), far_v, ((1,), (0,)))
        nearby = dot(softmax_dot(q, near_k, causal), near_v, ((1,), (0,)))
        return (g * remote + (1.0 - g) * nearby).astype(BF16)

    out = lax.map(
        one_head,
        (by_head(queries), fetch(mem_keys), fetch(mem_values), by_head(local_keys), by_head(local_values), gate),
    )
    combined = out.transpose(1, 0, 2).reshape(queries.shape)
    partial = jnp.dot(combined, out_weight, preferred_element_type=F32)
    return lax.psum_scatter(partial, "tp", scatter_dimension=0, tiled=True).astype(BF16)


def per_device(
    queries, local_keys, local_values, mem_keys, mem_values, gate_bias, out_weight, block_ids, block_home
):
    gate = jax.nn.sigmoid(gate_bias)
    ids = block_ids.transpose(1, 2, 0).reshape(2, HL, TOPK, PLANES * SIDE)
    home = block_home.reshape(8, 128)
    own0, lists, address, over = start(mem_keys, mem_values, ids, home)
    attention = (gate, mem_keys, mem_values, queries, local_keys, local_values, out_weight)
    return lax.cond(
        over[0, 0] <= 0.5,
        lambda: fast_path(own0, lists, address, ids, home, *attention),
        lambda: slow_path(*attention, block_ids, block_home),
    )


def solution(mesh):
    in_specs = (
        P("mem", "tp"), P("mem", "tp"), P("mem", "tp"), P("mem", "tp"), P("mem", "tp"),
        P("tp"), P("tp", None), P(), P(),
    )
    return jax.shard_map(
        per_device, mesh=mesh, in_specs=in_specs, out_specs=P(("mem", "tp"), None), check_vma=False
    )
```

```python
import functools
import math

import jax
import jax.numpy as jnp
from jax import lax
from jax.experimental import pallas as pl
from jax.experimental.pallas import tpu as pltpu
from jax.sharding import PartitionSpec as P

HD = 128
BLK = 128
TOPK = 16
PLANES = 8
SIDE = 16
HL = 8
GROUPS = 2
HG = HL // GROUPS
MB = 8
ROWS = BLK // SIDE
OWN = SIDE * MB * HG
CAPS = (328, 268, 188, 88)
OFFS = (0, 328, 596, 784)
CSUM = 872
CUTS = (0, 88, 188, 268, 328)
NPIECE = OWN + 2 * CSUM
PIECE = 2 * ROWS
LPAD = 384
SLOTS = HG * TOPK
MESH = pl.DeviceIdType.MESH
F32 = jnp.float32
BF16 = jnp.bfloat16
SCALE = math.log2(math.e) / math.sqrt(HD)


def iota(shape, axis):
    return lax.broadcasted_iota(jnp.int32, shape, axis)


def hot(mask):
    return jnp.where(mask, 1.0, 0.0).astype(BF16)


def dot(a, b, dims):
    return lax.dot_general(a, b, (dims, ((), ())), preferred_element_type=F32)


def find(ids_ref, home_ref, side, h):
    home = home_ref[...]
    home = jnp.concatenate([home >> 5, home & 31], axis=0).astype(F32).astype(BF16)
    block = ids_ref[side, h]
    ids = jnp.concatenate([block[q : q + 1] for q in range(TOPK)], axis=1)
    both = dot(home, hot(iota((128, 2048), 0) == (ids & 127)), ((1,), (0,)))
    at_hi = iota((8, 2048), 0) == (ids >> 7)
    pos_hi = jnp.sum(jnp.where(at_hi, both[:8], 0.0), axis=0, keepdims=True).astype(jnp.int32)
    pos_lo = jnp.sum(jnp.where(at_hi, both[8:], 0.0), axis=0, keepdims=True).astype(jnp.int32)
    return hot(iota((32, 2048), 0) == pos_hi), pos_lo


def plan_requests(ids_ref, home_ref, address_ref, dest_ref, tp):
    def one_dest(h, carry):
        by_hi, pos_lo = find(ids_ref, home_ref, tp, h)
        found = dot(address_ref[h].astype(BF16), by_hi, ((1,), (0,)))
        at_lo = iota((32, 2048), 0) == pos_lo
        dest_hi = jnp.sum(jnp.where(at_lo, found[:32], 0.0), axis=0, keepdims=True)
        dest_lo = jnp.sum(jnp.where(at_lo, found[32:], 0.0), axis=0, keepdims=True)
        dest = (dest_hi * 32.0 + dest_lo).astype(jnp.int32)
        rows = jnp.concatenate([dest[:, q * 128 : q * 128 + 128] for q in range(TOPK)], axis=0)
        dest_ref[pl.ds(pl.multiple_of(h * TOPK, TOPK), TOPK), :] = rows
        return carry

    lax.fori_loop(0, HL, one_dest, 0)


def plan_ring(ids_ref, home_ref, lists_ref, address_ref, over_ref, rank_s, plane, tp):
    lane = iota((1, 2048), 1)
    plane_term = ((lane & 127) >> 4) * 32
    row_plane = iota((32, 256), 0) >> 2
    even = (iota((32, 256), 1) & 1) == 0
    dz = ((iota((32, 256), 1) >> 5) - row_plane) & 7
    reach = (jnp.where(dz <= 3, dz, 0), jnp.where(dz >= 5, 8 - dz, 0), jnp.where(dz == 4, 4, 0))

    r, s = iota((256, 256), 0), iota((256, 256), 1)
    same_group = (r >> 7) == (s >> 7)
    prefix = hot(same_group & (r <= s))
    whole = hot(same_group)
    same_plane = (r >> 2) == (s >> 2)
    rows_before = hot(same_plane & (s < r))
    rows_all = hot(same_plane)
    over = jnp.zeros((32, 256), F32)
    ranks, full = [], []
    for other in range(2):
        side = tp if other == 0 else 1 - tp

        def one_head(h, far):
            by_hi, pos_lo = find(ids_ref, home_ref, side, h)
            count = dot(by_hi, hot(iota((256, 2048), 0) == plane_term + pos_lo), ((1,), (1,)))
            out = []
            for way in range(3):
                value = jnp.where(count > 0.5, reach[way], 0)
                for shift in (128, 64, 32):
                    value = jnp.maximum(value, pltpu.roll(value, shift, 1))
                out.append(jnp.where((iota((32, 256), 1) >> 5) == h, value, far[way]))
            return tuple(out)

        zero = jnp.zeros((32, 256), jnp.int32)
        up, down, opposite = lax.fori_loop(0, HL, one_head, (zero, zero, zero))
        upward = (up > down) | ((up == down) & even)
        far = (
            jnp.where(upward, jnp.maximum(up, opposite), up),
            jnp.where(upward, down, jnp.maximum(down, opposite)),
        )
        levels = jnp.concatenate(
            [jnp.where(far[way] == d, 1.0, 0.0) for way in range(2) for d in (4, 3, 2, 1)], axis=0
        )
        level_hot = levels.astype(BF16)
        before_lane = dot(level_hot, prefix, ((1,), (0,)))
        row_total = dot(level_hot, whole, ((1,), (0,))).astype(BF16)
        before_row = dot(rows_before, row_total, ((1,), (0,)))
        plane_total = dot(rows_all, row_total, ((1,), (0,)))
        for way in range(2):
            base = jnp.zeros((32, 256), F32)
            rank = jnp.zeros((32, 256), F32)
            for e in range(4):
                part = slice((way * 4 + e) * 32, (way * 4 + e) * 32 + 32)
                rank = rank + levels[part] * (base + before_row[part] + before_lane[part])
                base = base + plane_total[part]
                over = jnp.maximum(over, base - float(CAPS[3 - e]))
            if other == 0:
                full.append(far[way] == 4)
                ranks.append(rank.astype(jnp.int32) - 1)
                for p in range(PLANES):
                    rank_s[way, p] = ranks[way][p * 4 : p * 4 + 4]
    over_ref[...] = jnp.broadcast_to(jnp.max(over, keepdims=True), (8, 128))

    values = jnp.where(iota((8, 128), 0) == 0, iota((8, 128), 1), 1).astype(F32).astype(BF16)
    for way in range(2):
        mine = rank_s[way, plane]
        for g in range(GROUPS):
            index = jnp.zeros((1, LPAD), F32)
            for rr in range(4):
                wanted = mine[rr : rr + 1, g * 128 : g * 128 + 128]
                got = dot(values, hot(iota((LPAD, 128), 0) == wanted), ((1,), (1,)))
                index = index + got[0:1] + got[1:2] * float(rr * 128)
            lists_ref[g * 2 + way : g * 2 + way + 1, :] = index.astype(jnp.int32)

    dz = (plane - row_plane) & 7
    up = ((dz >= 1) & (dz <= 3)) | ((dz == 4) & full[0])
    down = (dz >= 5) | ((dz == 4) & full[1])
    address = (iota((32, 256), 0) & 3) * 128 + (iota((32, 256), 1) & 127)
    for d in range(1, 5):
        address = jnp.where(up & (dz == d), ranks[0] + (OWN + OFFS[d - 1]), address)
        address = jnp.where(down & (8 - dz == d), ranks[1] + (OWN + CSUM + OFFS[d - 1]), address)
    high = jnp.transpose((address >> 5).astype(F32))
    low = jnp.transpose((address & 31).astype(F32))
    for h in range(HL):
        part = slice(h * 32, h * 32 + 32)
        address_ref[h] = jnp.concatenate([high[part], low[part]], axis=0)


def pick_list(g, lists_ref, own, out):
    for way in range(2):

        def one(j, carry):
            out[way * CAPS[0] + j] = own[lists_ref[g * 2 + way, j]]
            return carry

        lax.fori_loop(0, CAPS[0], one, 0, unroll=41)


def pick_requests(g, r, dest_ref, pool, out):
    column = (lax.axis_index("mem") // SIDE) * SIDE + r

    for j in range(SLOTS):
        out[r * SLOTS + j] = pool[dest_ref[g * SLOTS + j, column]]


def pick(name, list_group, request_group, lists, dest, own_next, own, ring):
    smem = pl.BlockSpec(memory_space=pltpu.SMEM)
    hbm = pl.BlockSpec(memory_space=pl.ANY)
    with_list, with_requests = own_next is not None, own is not None
    steps = 4

    def kernel(*refs):
        refs = list(refs)
        lists_ref, dest_ref = refs.pop(0), refs.pop(0)
        next_hbm = refs.pop(0) if with_list else None
        own_hbm, ring_hbm = (refs.pop(0), refs.pop(0)) if with_requests else (None, None)
        list_hbm = refs.pop(0) if with_list else None
        given_hbm = refs.pop(0) if with_requests else None
        out_sem, in_sem = refs.pop(), refs.pop()
        if with_list:
            next_v, list_v = refs.pop(0), refs.pop(0)
            next_in = pltpu.make_async_copy(next_hbm, next_v, in_sem.at[0])
            next_in.start()
        if with_requests:
            pool_v, given_v = refs.pop(0), refs.pop(0)
            own_in = pltpu.make_async_copy(own_hbm, pool_v.at[pl.ds(0, OWN)], in_sem.at[1])
            cut = CSUM // 2
            ring_in = [
                pltpu.make_async_copy(
                    ring_hbm.at[pl.ds(n * cut, cut)], pool_v.at[pl.ds(OWN + n * cut, cut)], in_sem.at[2 + n]
                )
                for n in range(4)
            ]
            for copy in ring_in + [own_in]:
                copy.start()
        outs = []
        if with_list:
            next_in.wait()
            pick_list(list_group, lists_ref, next_v, list_v)
            outs.append(pltpu.make_async_copy(list_v, list_hbm, out_sem.at[steps]))
            outs[-1].start()
        if with_requests:
            for copy in ring_in + [own_in]:
                copy.wait()
            for step in range(steps):
                wide = SIDE // steps

                def one(r, carry):
                    pick_requests(request_group, r, dest_ref, pool_v, given_v)
                    return carry

                lax.fori_loop(step * wide, step * wide + wide, one, 0)
                part = pl.ds(step * wide * SLOTS, wide * SLOTS)
                outs.append(pltpu.make_async_copy(given_v.at[part], given_hbm.at[part], out_sem.at[step]))
                outs[-1].start()
        for out in outs:
            out.wait()

    def piece(count):
        return (count, PIECE, HD)

    shapes, scratch, data = [], [], []
    if with_list:
        shapes.append(jax.ShapeDtypeStruct(piece(2 * CAPS[0]), BF16))
        scratch += [pltpu.VMEM(piece(OWN), BF16), pltpu.VMEM(piece(2 * CAPS[0]), BF16)]
        data.append(own_next)
    if with_requests:
        shapes.append(jax.ShapeDtypeStruct(piece(SIDE * SLOTS), BF16))
        scratch += [pltpu.VMEM(piece(NPIECE), BF16), pltpu.VMEM(piece(SIDE * SLOTS), BF16)]
        data += [own, ring]
    return pl.pallas_call(
        kernel,
        out_shape=tuple(shapes),
        in_specs=[smem, smem] + [hbm] * len(data),
        out_specs=tuple([hbm] * len(shapes)),
        scratch_shapes=scratch + [pltpu.SemaphoreType.DMA((6,)), pltpu.SemaphoreType.DMA((steps + 1,))],
        compiler_params=pltpu.CompilerParams(vmem_limit_bytes=(24 if with_requests else 10) << 20),
        name=name,
    )(lists, dest, *data)


def place():
    mem = lax.axis_index("mem")
    plane, me = mem // SIDE, mem % SIDE
    above = ((plane + 1) % PLANES) * SIDE + me
    below = ((plane + PLANES - 1) % PLANES) * SIDE + me
    return plane, me, lax.axis_index("tp"), (above, below)


def peer_of(me, k):
    step = (k * 7) % SIDE
    return ((me // 4 + step // 4) % 4) * 4 + (me % 4 + step % 4) % 4


def greet(ring, partner):
    plane, me, tp, nexts = place()
    barrier = pltpu.get_barrier_semaphore()

    def one(k, carry):
        peer = plane * SIDE + peer_of(me, k)
        pl.semaphore_signal(barrier, inc=1, device_id=(peer, tp), device_id_type=MESH)
        return carry

    lax.fori_loop(1, SIDE, one, 0)
    count = SIDE - 1
    if ring:
        for peer in nexts:
            pl.semaphore_signal(barrier, inc=1, device_id=(peer, tp), device_id_type=MESH)
        count += 2
    if partner:
        pl.semaphore_signal(
            barrier, inc=1, device_id=(plane * SIDE + me, 1 - tp), device_id_type=MESH
        )
        count += 1
    pl.semaphore_wait(barrier, count)


def spread(g, sources, own, send, recv):
    plane, me, tp, _ = place()
    base = (me // 4) * 128 + (me % 4) * MB

    def parts(i):
        for h in range(HG):
            for kv in range(2):
                yield (
                    sources[kv].at[:, i, :, pl.ds((g * HG + h) * HD, HD)],
                    own.at[pl.ds(base + h * 32, MB), pl.ds(kv * ROWS, ROWS)],
                )

    def to_peer(k, carry):
        i = peer_of(me, k)
        for source, target in parts(i):
            pltpu.make_async_remote_copy(
                src_ref=source,
                dst_ref=target,
                send_sem=send,
                recv_sem=recv,
                device_id=(plane * SIDE + i, tp),
                device_id_type=MESH,
            ).start()
        return carry

    lax.fori_loop(1, SIDE, to_peer, 0)
    for source, target in parts(me):
        pltpu.make_async_copy(source, target, recv).start()


def spread_wait(own, send, recv):
    pltpu.make_async_copy(own, own, recv).wait()
    sent = own.at[pl.ds(0, (SIDE - 1) * HG * MB)]
    pltpu.make_async_copy(sent, sent, send).wait()


def hop_copy(lst, ring, send, recv, way, part, d):
    _, _, tp, nexts = place()
    low, count = CUTS[part], CUTS[part + 1] - CUTS[part]
    base = way * CSUM + low
    if d == 0:
        source = lst.at[pl.ds(way * CAPS[0] + low, count)]
    else:
        source = ring.at[pl.ds(base + OFFS[d - 1], count)]
    return pltpu.make_async_remote_copy(
        src_ref=source,
        dst_ref=ring.at[pl.ds(base + OFFS[d], count)],
        send_sem=send.at[way, part, d],
        recv_sem=recv.at[way, part, d],
        device_id=(nexts[way], tp),
        device_id_type=MESH,
    )


def hop_first(args):
    for part in range(4):
        for way in range(2):
            hop_copy(*args, way, part, 0).start()


def hop_on(args, d):
    for part in range(4 - d):
        for way in range(2):
            hop_copy(*args, way, part, d - 1).wait_recv()
            hop_copy(*args, way, part, d).start()


def hop_last(args):
    for part in range(4):
        for way in range(2):
            hop_copy(*args, way, part, 3 - part).wait_recv()
            for d in range(4 - part):
                hop_copy(*args, way, part, d).wait_send()


def deliver(given, rcv, send, recv):
    plane, me, tp, _ = place()
    for h in range(HG):

        def to_peer(k, carry):
            i = peer_of(me, k)
            pltpu.make_async_remote_copy(
                src_ref=given.at[pl.ds(i * SLOTS + h * TOPK, TOPK)],
                dst_ref=rcv.at[h, me],
                send_sem=send,
                recv_sem=recv.at[h],
                device_id=(plane * SIDE + i, tp),
                device_id_type=MESH,
            ).start()
            return carry

        lax.fori_loop(1, SIDE, to_peer, 0)
        pltpu.make_async_copy(
            given.at[pl.ds(me * SLOTS + h * TOPK, TOPK)], rcv.at[h, me], recv.at[h]
        ).start()


def deliver_sent(given, send):
    sent = given.at[pl.ds(0, (SIDE - 1) * SLOTS)]
    pltpu.make_async_copy(sent, sent, send).wait()


def softmax_dot(query, keys, visible):
    scores = dot(query, keys, ((1,), (1,)))
    if visible is not None:
        scores = jnp.where(visible, scores, -1e30)
    highest = jnp.max(scores, axis=1, keepdims=True)
    exponent = jnp.exp2((scores - highest) * SCALE)
    return (exponent * (1.0 / jnp.sum(exponent, axis=1, keepdims=True))).astype(BF16)


def columns(h):
    return pl.ds(pl.multiple_of(h * HD, HD), HD)


def attend_near(g, q_ref, k_ref, v_ref, near):
    def one(h, carry):
        cols = columns(g * HG + h)
        for rb in range(4):
            rows = pl.ds(rb * 128, 128)
            width = (rb + 1) * 128
            visible = iota((128, width), 0) + rb * 128 >= iota((128, width), 1)
            part = softmax_dot(q_ref[rows, cols], k_ref[pl.ds(0, width), cols], visible)
            near[rows, columns(h)] = dot(part, v_ref[pl.ds(0, width), cols], ((1,), (0,)))
        return carry

    lax.fori_loop(0, HG, one, 0)


def attend_far(g, low, high, gate_ref, q_ref, rcv, recv, near, out_ref, done):
    def one(h, carry):
        pltpu.make_async_copy(rcv.at[h], rcv.at[h], recv.at[h]).wait()
        rows = rcv[h].astype(F32).reshape(SIDE * TOPK, PIECE, HD)
        keys = rows[:, :ROWS].reshape(SIDE * TOPK * ROWS, HD).astype(BF16)
        values = rows[:, ROWS:].reshape(SIDE * TOPK * ROWS, HD).astype(BF16)
        cols = columns(g * HG + h)
        gate = gate_ref[g * HG + h]

        def block(rb, inner):
            rows = pl.ds(pl.multiple_of(rb * 128, 128), 128)
            remote = dot(softmax_dot(q_ref[rows, cols], keys, None), values, ((1,), (0,)))
            mixed = gate * remote + (1.0 - gate) * near[rows, columns(h)]
            out_ref[rows, columns(h)] = mixed.astype(BF16)
            return inner

        lax.fori_loop(0, 4, block, 0)
        if done is not None:
            done(h)
        return carry

    lax.fori_loop(low, high, one, 0)


def kernel_spread(
    mem_keys, mem_values, ids_ref, home_ref, own, lists_ref, address_ref, over_ref, rank_s, send, recv
):
    plane, _, tp, _ = place()
    greet(False, False)
    spread(0, (mem_keys, mem_values), own, send, recv)
    plan_ring(ids_ref, home_ref, lists_ref, address_ref, over_ref, rank_s, plane, tp)
    spread_wait(own, send, recv)


def kernel_ring(
    mem_keys, mem_values, lst, ids_ref, home_ref, address_ref, ring, own_next, dest_ref, *sems
):
    s1_send, s1_recv, z_send, z_recv = sems
    args = (lst, ring, z_send, z_recv)
    greet(True, False)
    hop_first(args)
    spread(1, (mem_keys, mem_values), own_next, s1_send, s1_recv)
    for d in range(1, 4):
        hop_on(args, d)
    plan_requests(ids_ref, home_ref, address_ref, dest_ref, lax.axis_index("tp"))
    hop_last(args)
    spread_wait(own_next, s1_send, s1_recv)


def kernel_ring_attend(
    gate_ref, lst, given, weight, q_ref, k_ref, v_ref, ring, out_ref, other_weight, rcv, near, *sems
):
    z_send, z_recv, s3_send, s3_recv, w_sems = sems
    plane, me, tp, _ = place()
    args = (lst, ring, z_send, z_recv)
    far = (gate_ref, q_ref, rcv, s3_recv, near, out_ref, None)
    greet(True, True)
    hop_first(args)
    deliver(given, rcv, s3_send, s3_recv)
    swap = pltpu.make_async_remote_copy(
        src_ref=weight,
        dst_ref=other_weight,
        send_sem=w_sems.at[0],
        recv_sem=w_sems.at[1],
        device_id=(plane * SIDE + me, 1 - tp),
        device_id_type=MESH,
    )
    swap.start()
    attend_near(0, q_ref, k_ref, v_ref, near)
    hop_on(args, 1)
    attend_far(0, 0, 2, *far)
    hop_on(args, 2)
    attend_far(0, 2, HG, *far)
    hop_on(args, 3)
    hop_last(args)
    deliver_sent(given, s3_send)
    swap.wait()


def kernel_attend(
    gate_ref, given, half_ref, w_own, w_other, q_ref, k_ref, v_ref, out_ref,
    rcv, near, half, got, total, s3_send, s3_recv, half_send, half_recv,
):
    plane, me, tp, _ = place()
    rows = half_ref.shape[0] // 2
    mine = pl.ds(pl.multiple_of(tp * rows, rows), rows)
    theirs = pl.ds(pl.multiple_of((1 - tp) * rows, rows), rows)
    cut = HG * HD

    def swap(source, target, sem):
        return pltpu.make_async_remote_copy(
            src_ref=source,
            dst_ref=target,
            send_sem=half_send.at[sem],
            recv_sem=half_recv.at[sem],
            device_id=(plane * SIDE + me, 1 - tp),
            device_id_type=MESH,
        )

    def head_swap(h):
        return swap(half.at[theirs, columns(h)], got.at[1, :, columns(h)], 1 + h)

    greet(False, True)
    deliver(given, rcv, s3_send, s3_recv)
    first = swap(half_ref.at[theirs], got.at[0], 0)
    first.start()
    attend_near(1, q_ref, k_ref, v_ref, near)
    first.wait()

    def early(n, carry):
        cols = pl.ds(pl.multiple_of(n * 256, 256), 256)
        total[:, cols] = dot(half_ref[mine], w_own[:cut, cols], ((1,), (0,))) + dot(
            got[0], w_other[:cut, cols], ((1,), (0,))
        )
        return carry

    lax.fori_loop(0, out_ref.shape[1] // 256, early, 0)
    attend_far(
        1, 0, HG, gate_ref, q_ref, rcv, s3_recv, near, half, lambda h: head_swap(h).start()
    )
    for h in range(HG):
        head_swap(h).wait()

    def late(n, carry):
        cols = pl.ds(pl.multiple_of(n * 256, 256), 256)
        mixed = total[:, cols] + dot(half[mine], w_own[cut:, cols], ((1,), (0,)))
        mixed = mixed + dot(got[1], w_other[cut:, cols], ((1,), (0,)))
        out_ref[:, cols] = mixed.astype(BF16)
        return carry

    lax.fori_loop(0, out_ref.shape[1] // 256, late, 0)
    deliver_sent(given, s3_send)


SMEM = pl.BlockSpec(memory_space=pltpu.SMEM)
HBM = pl.BlockSpec(memory_space=pl.ANY)
VMEM = pl.BlockSpec(memory_space=pltpu.VMEM)


def call(kernel, name, number, mib, outs, in_specs, out_specs, scratch, *args):
    return pl.pallas_call(
        kernel,
        out_shape=outs,
        in_specs=in_specs,
        out_specs=out_specs,
        scratch_shapes=scratch,
        compiler_params=pltpu.CompilerParams(
            collective_id=number, has_side_effects=True, vmem_limit_bytes=mib << 20
        ),
        name=name,
    )(*args)


def shape(dims, dtype=BF16):
    return jax.ShapeDtypeStruct(dims, dtype)


def view(rows):
    return rows.reshape(MB, SIDE, ROWS, HL * HD)


def start(mem_keys, mem_values, ids, home):
    one = pltpu.SemaphoreType.DMA
    return call(
        kernel_spread, "spread", 0, 24,
        (
            shape((OWN, PIECE, HD)), shape((4, LPAD), jnp.int32),
            shape((HL, 64, 32), F32), shape((8, 128), F32),
        ),
        [HBM, HBM, VMEM, VMEM], (HBM, VMEM, VMEM, VMEM),
        [pltpu.VMEM((2, PLANES, 4, 256), jnp.int32), one, one],
        view(mem_keys), view(mem_values), ids, home,
    )


def fast_path(
    own0, lists, address, ids, home, gate,
    mem_keys, mem_values, queries, local_keys, local_values, out_weight,
):
    tokens = queries.shape[0]
    half = (tokens, HG * HD)
    ring_shape = shape((2 * CSUM, PIECE, HD))
    one = pltpu.SemaphoreType.DMA
    pair, heads, ring = one((2,)), one((HG,)), one((2, 4, 4))
    swaps = one((HG + 1,))
    rcv = pltpu.VMEM((HG, SIDE, TOPK, PIECE, HD), BF16)
    near = pltpu.VMEM(half, F32)
    (lst0,) = pick("pick_first", 0, None, lists, lists, own0, None, None)
    ring0, own1, dest = call(
        kernel_ring, "ring", 1, 16,
        (ring_shape, shape(own0.shape), shape((HL * TOPK, PLANES * SIDE), jnp.int32)),
        [HBM, HBM, HBM, VMEM, VMEM, VMEM], (HBM, HBM, VMEM), [one, one, ring, ring],
        view(mem_keys), view(mem_values), lst0, ids, home, address,
    )
    lst1, given0 = pick("pick_both", 1, 0, lists, dest, own1, own0, ring0)
    ring1, half0, other_weight = call(
        kernel_ring_attend, "ring_attend", 2, 28,
        (ring_shape, shape(half), shape(out_weight.shape)),
        [SMEM, HBM, HBM, HBM, VMEM, VMEM, VMEM], (HBM, VMEM, HBM),
        [rcv, near, ring, ring, one, heads, pair],
        gate, lst1, given0, out_weight, queries, local_keys, local_values,
    )
    (given1,) = pick("pick_last", None, 1, lists, dest, None, own1, ring1)
    return call(
        kernel_attend, "attend", 3, 36, shape((tokens // 2, out_weight.shape[1])),
        [SMEM, HBM, VMEM, VMEM, VMEM, VMEM, VMEM, VMEM], VMEM,
        [
            rcv, near, pltpu.VMEM(half, BF16), pltpu.VMEM((2, tokens // 2, HG * HD), BF16),
            pltpu.VMEM((tokens // 2, out_weight.shape[1]), F32), one, heads, swaps, swaps,
        ],
        gate, given1, half0, out_weight, other_weight, queries, local_keys, local_values,
    )


def rank_within(owner_row):
    request_count = owner_row.shape[0]
    order_index = jnp.arange(request_count, dtype=jnp.int32)
    earlier = order_index[:, None] > order_index[None, :]
    same_owner = owner_row[:, None] == owner_row[None, :]
    return jnp.sum((same_owner & earlier).astype(jnp.int32), axis=1)


def slow_path(
    gate, mem_keys, mem_values, queries, local_keys, local_values, out_weight, block_ids, block_home
):
    mem_count = lax.axis_size("mem")
    mem_index = lax.axis_index("mem")
    tp_index = lax.axis_index("tp")
    requests = HL * TOPK
    slots = 2
    group_ids = lax.dynamic_slice_in_dim(block_ids, tp_index * HL, HL, 1).reshape(mem_count, requests)
    home_slots = jnp.take(block_home, group_ids, axis=0)
    owners = home_slots // MB
    codes = (home_slots % MB) * HL + jnp.arange(requests, dtype=jnp.int32)[None, :] // TOPK
    own_owners = lax.dynamic_index_in_dim(owners, mem_index, 0, keepdims=False)
    own_codes = lax.dynamic_index_in_dim(codes, mem_index, 0, keepdims=False)
    own_ranks = rank_within(own_owners)
    slot_index = jnp.arange(slots, dtype=jnp.int32)
    owner_index = jnp.arange(mem_count, dtype=jnp.int32)
    matches = (own_owners[None, None, :] == owner_index[:, None, None]) & (
        own_ranks[None, None, :] == slot_index[None, :, None]
    )
    table = jnp.sum(jnp.where(matches, own_codes[None, None, :], 0), axis=2)
    wanted = lax.all_to_all(table, "mem", split_axis=0, concat_axis=0, tiled=True)
    flat_slot = own_owners * slots + own_ranks

    def fetch(rows):
        blocks = rows.reshape(MB, BLK, HL, HD)
        sent = blocks[wanted // HL, :, wanted % HL, :]
        got = lax.all_to_all(sent, "mem", split_axis=0, concat_axis=0, tiled=True)
        far = jnp.take(got.reshape(mem_count * slots, BLK, HD), flat_slot, axis=0)
        return far.reshape(HL, TOPK * BLK, HD)

    positions = jnp.arange(queries.shape[0], dtype=jnp.int32)
    causal = positions[:, None] >= positions[None, :]

    def by_head(x):
        return x.reshape(x.shape[0], HL, HD).transpose(1, 0, 2)

    def one_head(parts):
        q, far_k, far_v, near_k, near_v, g = parts
        remote = dot(softmax_dot(q, far_k, None), far_v, ((1,), (0,)))
        nearby = dot(softmax_dot(q, near_k, causal), near_v, ((1,), (0,)))
        return (g * remote + (1.0 - g) * nearby).astype(BF16)

    out = lax.map(
        one_head,
        (by_head(queries), fetch(mem_keys), fetch(mem_values), by_head(local_keys), by_head(local_values), gate),
    )
    combined = out.transpose(1, 0, 2).reshape(queries.shape)
    partial = jnp.dot(combined, out_weight, preferred_element_type=F32)
    return lax.psum_scatter(partial, "tp", scatter_dimension=0, tiled=True).astype(BF16)


def per_device(
    queries, local_keys, local_values, mem_keys, mem_values, gate_bias, out_weight, block_ids, block_home
):
    gate = jax.nn.sigmoid(gate_bias)
    ids = block_ids.transpose(1, 2, 0).reshape(2, HL, TOPK, PLANES * SIDE)
    home = block_home.reshape(8, 128)
    own0, lists, address, over = start(mem_keys, mem_values, ids, home)
    attention = (gate, mem_keys, mem_values, queries, local_keys, local_values, out_weight)
    return lax.cond(
        over[0, 0] <= 0.5,
        lambda: fast_path(own0, lists, address, ids, home, *attention),
        lambda: slow_path(*attention, block_ids, block_home),
    )


def solution(mesh):
    in_specs = (
        P("mem", "tp"), P("mem", "tp"), P("mem", "tp"), P("mem", "tp"), P("mem", "tp"),
        P("tp"), P("tp", None), P(), P(),
    )
    return jax.shard_map(
        per_device, mesh=mesh, in_specs=in_specs, out_specs=P(("mem", "tp"), None), check_vma=False
    )
```
